128 devices in a mesh: graph: 32 (over y, x, core), dp: 4 (over z).
Axes of the slice: x: 4, y: 4, z: 4, core: 2. Of those that a mesh axis runs over, the one named last changes fastest.
Arguments:
- grid_latent: bfloat16 [4, 16384, 512], P('dp', 'graph'), may hold values from -6 to 6
- mesh_embed: bfloat16 [8192, 512], P('graph'), may hold values from -6 to 6
- mesh_edges: bfloat16 [49152, 512], P('graph'), may hold values from -6 to 6
- edge_geometry: bfloat16 [32, 4, 2048], P('graph'), may hold values from -6 to 6
- edge_counts: int32 [32, 32], P('graph'), may hold values from 0 to 64, as said below
- edge_sources: int32 [32, 2048], P('graph'), may hold values from 0 to 511
- edge_targets: int32 [32, 2048], P('graph'), may hold values from 0 to 255
- halo_sources: int32 [32, 128], P('graph'), may hold values from 0 to 255
- mesh_sources: int32 [32, 1536], P('graph'), may hold values from 0 to 383, as said below
- mesh_targets: int32 [32, 1536], P('graph'), may hold values from 0 to 255
- grid_weight: bfloat16 [512, 512], replicated, may hold values from -0.25 to 0.25
- geometry_weight: float32 [4, 512], replicated, may hold values from -3 to 3
- message_weight: bfloat16 [512, 512], replicated, may hold values from -0.25 to 0.25
- mesh_update: bfloat16 [1024, 512], replicated, may hold values from -0.1875 to 0.1875
- mesh_output: bfloat16 [512, 512], replicated, may hold values from -0.25 to 0.25
- processor: bfloat16 [2, 3584, 512], replicated, may hold values from -0.15625 to 0.15625
- cotangent: bfloat16 [4, 8192, 512], P('dp', 'graph'), may hold values from -6 to 6
Outputs:
- mesh_result: bfloat16 [4, 8192, 512], P('dp', 'graph')
- mesh_gradient: bfloat16 [4, 8192, 512], P('dp', 'graph')
- gradients: bfloat16 [2, 3584, 512], replicated
The draws below stay inside these ranges and needn't reach their ends.
Inputs may be any that keep to these rules, and one draw needn't show every extreme that they name: Slots of device s for device d beyond edge_counts[s, d] are empty; every device fills all 64 slots for itself, and every device fills all 64 slots for one common device. `edge_sources`: row s holds local grid rows of device s. `edge_targets`: row d holds local mesh rows of device d, for slot c from device s at column s * 64 + c. `halo_sources`: row s, columns d * 4 to d * 4 + 3 are the local rows that device s sends to device d; every device sends 4 rows to every device, itself included. `mesh_sources`: A value under 256 is a local row; a value 256 + s * 4 + k is halo slot k from device s.
All inputs are finite; a program needn't handle non-finite values.
Results may differ from the reference program's by a relative error of at most 0.024.
Values may be sent and summed in bfloat16 or wider, within the bound.
A program may use at most 128 MiB of HBM per device.

```python
import math
import jax
import jax.numpy as jnp
from jax import lax

D = 512
GD = 512
MD = 256
EMD = 1536
CAP = 64
HB = 4
L = 2
SAMPLES = 4
GRID = 16384
MESH = 8192
EDGES = 49152
N_GRAPH = 32
N_DP = 4


def draw_edge_counts(key, part):
    nearby_key, distant_key, hottest_key = jax.random.split(jax.random.fold_in(key, 11), 3)
    peers = N_GRAPH
    nearby_counts = jax.random.randint(nearby_key, (peers, peers), CAP // 2, CAP + 1)
    distant_counts = jax.random.randint(distant_key, (peers, peers), CAP // 4, CAP // 2 + 1)
    source = jnp.arange(peers, dtype=jnp.int32)[:, None]
    target = jnp.arange(peers, dtype=jnp.int32)[None, :]
    offset = (target - source) % peers
    nearby = (offset == 1) | (offset == 2) | (offset == peers - 1)
    counts = jnp.where(nearby, nearby_counts, distant_counts)
    hottest = jax.random.randint(hottest_key, (), 0, peers)
    counts = jnp.where((offset == 0) | (target == hottest), CAP, counts)
    return counts.astype(jnp.int32)


def draw_mesh_sources(key, part):
    local_key, remote_key, choose_key = jax.random.split(jax.random.fold_in(key, 23), 3)
    extent = (N_GRAPH, EMD)
    local_rows = jax.random.randint(local_key, extent, 0, MD)
    remote_rows = jax.random.randint(remote_key, extent, MD, MD + N_GRAPH * HB)
    remote = jax.random.randint(choose_key, extent, 0, 4) == 0
    return jnp.where(remote, remote_rows, local_rows).astype(jnp.int32)


def with_ends(values, stream_key, smallest, high):
    shape = values.shape
    place = [jax.random.randint(jax.random.fold_in(stream_key, axis), (), 0, shape[axis]) for axis in range(len(shape))]
    values = values.at[tuple(place)].set(smallest)
    longest = shape.index(max(shape))
    place[longest] = (place[longest] + 1) % shape[longest]
    return values.at[tuple(place)].set(high)


def level_of(own_key, shape, cuts, low, largest):
    loudness, own = 1.0, jax.random.fold_in(own_key, 6)
    for axis_at, parts in cuts:
        draws = jnp.exp(jax.random.uniform(jax.random.fold_in(own, axis_at), (parts,), jnp.float32, low / len(cuts), largest / len(cuts)))
        loudness = loudness * jnp.repeat(draws, shape[axis_at] // parts).reshape([-1 if axis == axis_at else 1 for axis in range(len(shape))])
    return loudness


def noise(rng, shape, spread, limit, cuts=(), held_as=jnp.bfloat16):
    entries = jax.random.normal(rng, shape, jnp.float32) * spread
    if len(cuts) > 0:
        entries = level_of(rng, shape, cuts, -0.22, 0.18) * entries
    return jnp.clip(entries, min=-limit, max=limit).astype(held_as)


def setup_inputs(seed: int = 0) -> dict:
    key_of = jax.random.split(jax.random.key(seed), 18)
    grid_latent = noise(key_of[0], (SAMPLES, GRID, D), 1.0, 6.0, ((0, 4), (1, 32)))
    mesh_embed = noise(key_of[1], (MESH, D), 1.0, 6.0, ((0, 32),))
    mesh_edges = noise(key_of[2], (EDGES, D), 1.0, 6.0, ((0, 32),))
    edge_geometry = noise(key_of[3], (N_GRAPH, 4, N_GRAPH * CAP), 1.0, 6.0, ((0, 32),))
    edge_counts = draw_edge_counts(jax.random.fold_in(key_of[17], 71), 0)
    edge_sources = with_ends(jax.random.randint(key_of[5], (N_GRAPH, N_GRAPH * CAP), 0, GD), jax.random.fold_in(key_of[5], 1), 0, GD - 1).astype(jnp.int32)
    edge_targets = with_ends(jax.random.randint(key_of[6], (N_GRAPH, N_GRAPH * CAP), 0, MD), jax.random.fold_in(key_of[6], 1), 0, MD - 1).astype(jnp.int32)
    halo_sources = with_ends(jax.random.randint(key_of[7], (N_GRAPH, N_GRAPH * HB), 0, MD), jax.random.fold_in(key_of[7], 1), 0, MD - 1).astype(jnp.int32)
    mesh_sources = draw_mesh_sources(jax.random.fold_in(key_of[17], 71), 0)
    mesh_targets = with_ends(jax.random.randint(key_of[9], (N_GRAPH, EMD), 0, MD), jax.random.fold_in(key_of[9], 1), 0, MD - 1).astype(jnp.int32)
    grid_weight = noise(key_of[10], (D, D), D ** -0.5, 0.25)
    geometry_weight = noise(key_of[11], (4, D), 4 ** -0.5, 3.0, (), jnp.float32)
    message_weight = noise(key_of[12], (D, D), D ** -0.5, 0.25)
    mesh_update = noise(key_of[13], (2 * D, D), (2 * D) ** -0.5, 0.1875)
    mesh_output = noise(key_of[14], (D, D), D ** -0.5, 0.25)
    processor = noise(key_of[15], (L, 7 * D, D), (3 * D) ** -0.5, 0.15625)
    cotangent = noise(key_of[16], (SAMPLES, MESH, D), 1.0, 6.0, ((0, 4), (1, 32)))
    return {"grid_latent": grid_latent, "mesh_embed": mesh_embed, "mesh_edges": mesh_edges, "edge_geometry": edge_geometry, "edge_counts": edge_counts, "edge_sources": edge_sources, "edge_targets": edge_targets, "halo_sources": halo_sources, "mesh_sources": mesh_sources, "mesh_targets": mesh_targets, "grid_weight": grid_weight, "geometry_weight": geometry_weight, "message_weight": message_weight, "mesh_update": mesh_update, "mesh_output": mesh_output, "processor": processor, "cotangent": cotangent}


EPSILON = 1e-05
HIGHEST = lax.Precision.HIGHEST

def matmul(left, right):
    return jnp.dot(left, right, preferred_element_type=jnp.float32)

def weight_grad(left, right):
    return lax.dot_general(left, right, (((0,), (0,)), ((), ())), preferred_element_type=jnp.float32)

def input_grad(left, right):
    return lax.dot_general(left, right, (((1,), (1,)), ((), ())), preferred_element_type=jnp.float32)

def normalize(values):
    center = lax.optimization_barrier(jnp.mean(values, axis=-1, keepdims=True))
    shifted = values - center
    inverse = lax.rsqrt(lax.optimization_barrier(jnp.mean(shifted * shifted, axis=-1, keepdims=True)) + EPSILON)
    return (shifted * inverse, inverse)

def normalize_back(normed, inverse, upstream):
    first_mean = lax.optimization_barrier(jnp.mean(upstream, axis=-1, keepdims=True))
    second_mean = lax.optimization_barrier(jnp.mean(upstream * normed, axis=-1, keepdims=True))
    return inverse * (upstream - first_mean - normed * second_mean)

def swish_slope(values):
    sigma = jax.nn.sigmoid(values)
    return sigma * (1.0 + values * (1.0 - sigma))

def encode(grid_rows, mesh_embed, edge_geometry, edge_counts, edge_sources, edge_targets, grid_weight, geometry_weight, message_weight, mesh_update, mesh_output):
    width = mesh_embed.shape[1]
    peers = edge_counts.shape[0]
    slots = edge_sources.shape[1]
    capacity = slots // peers
    device = jnp.arange(peers).astype(jnp.int32)[:, None]
    position = jnp.arange(slots).astype(jnp.int32)[None, :]
    target_peer = position // capacity
    column = position % capacity
    senders = (device * GD + edge_sources).reshape(-1)
    targets = (target_peer * MD + edge_targets[target_peer, device * capacity + column]).reshape(-1)
    live = (column < edge_counts[device, target_peer]).reshape(-1)
    geometry = jnp.transpose(edge_geometry.astype(jnp.float32), (1, 0, 2)).reshape(4, -1)
    geometry_term = jnp.einsum('fs,fd->sd', geometry, geometry_weight, precision=HIGHEST)
    grid_proj = matmul(grid_rows, grid_weight)
    messages = jnp.where(live[:, None], jax.nn.silu(grid_proj[senders] + geometry_term), 0.0).astype(jnp.bfloat16)
    hidden_sum = jax.ops.segment_sum(messages.astype(jnp.float32), targets, num_segments=MESH).astype(jnp.bfloat16)
    aggregate = matmul(hidden_sum, message_weight).astype(jnp.bfloat16)
    pre_update = matmul(mesh_embed, mesh_update[:width]) + matmul(aggregate, mesh_update[width:])
    normed, inverse = normalize(matmul(jax.nn.silu(pre_update).astype(jnp.bfloat16), mesh_output))
    return (mesh_embed.astype(jnp.float32) + normed).astype(jnp.bfloat16)

def mesh_indices(halo_sources, mesh_sources, mesh_targets):
    peers = mesh_sources.shape[0]
    device = jnp.arange(peers).astype(jnp.int32)[:, None]
    local = mesh_sources < MD
    halo_slot = jnp.maximum(mesh_sources - MD, 0)
    source = halo_slot // HB
    within = halo_slot % HB
    remote_rows = halo_sources[source, device * HB + within]
    senders = jnp.where(local, device * MD + mesh_sources, source * MD + remote_rows).reshape(-1)
    receivers = (device * MD + mesh_targets).reshape(-1)
    return (senders.astype(jnp.int32), receivers.astype(jnp.int32))

def layer_forward(nodes, edges, senders, receivers, weights):
    width = nodes.shape[1]
    send_proj = matmul(nodes, weights[width:2 * width])
    recv_proj = matmul(nodes, weights[2 * width:3 * width])
    pre_edge = matmul(edges, weights[:width]) + send_proj[senders] + recv_proj[receivers]
    hidden_edge = jax.nn.silu(pre_edge).astype(jnp.bfloat16)
    normed_edge, inverse_edge = normalize(matmul(hidden_edge, weights[3 * width:4 * width]))
    new_edges = (edges.astype(jnp.float32) + normed_edge).astype(jnp.bfloat16)
    summed = jax.ops.segment_sum(new_edges.astype(jnp.float32), receivers, num_segments=MESH).astype(jnp.bfloat16)
    pre_node = matmul(nodes, weights[4 * width:5 * width]) + matmul(summed, weights[5 * width:6 * width])
    hidden_node = jax.nn.silu(pre_node).astype(jnp.bfloat16)
    normed_node, inverse_node = normalize(matmul(hidden_node, weights[6 * width:]))
    new_nodes = (nodes.astype(jnp.float32) + normed_node).astype(jnp.bfloat16)
    saved = (pre_edge, hidden_edge, normed_edge, inverse_edge, summed, pre_node, hidden_node, normed_node, inverse_node)
    return (new_nodes, new_edges, saved)

def layer_backward(nodes, edges, senders, receivers, weights, saved, grad_nodes, grad_edges):
    width = nodes.shape[1]
    pre_edge, hidden_edge, normed_edge, inverse_edge, summed, pre_node, hidden_node, normed_node, inverse_node = saved
    q_node = normalize_back(normed_node, inverse_node, grad_nodes).astype(jnp.bfloat16)
    grad_node_second = weight_grad(hidden_node, q_node)
    d_node = (input_grad(q_node, weights[6 * width:]) * swish_slope(pre_node)).astype(jnp.bfloat16)
    grad_node_own = weight_grad(nodes, d_node)
    grad_node_sum = weight_grad(summed, d_node)
    grad_summed = input_grad(d_node, weights[5 * width:6 * width])
    edge_upstream = grad_edges + grad_summed[receivers]
    q_edge = normalize_back(normed_edge, inverse_edge, edge_upstream).astype(jnp.bfloat16)
    grad_edge_second = weight_grad(hidden_edge, q_edge)
    d_edge = input_grad(q_edge, weights[3 * width:4 * width]) * swish_slope(pre_edge)
    d_edge16 = d_edge.astype(jnp.bfloat16)
    grad_send = jax.ops.segment_sum(d_edge, senders, num_segments=MESH).astype(jnp.bfloat16)
    grad_recv = jax.ops.segment_sum(d_edge, receivers, num_segments=MESH).astype(jnp.bfloat16)
    partial_value = jnp.concatenate([weight_grad(edges, d_edge16), weight_grad(nodes, grad_send), weight_grad(nodes, grad_recv), grad_edge_second, grad_node_own, grad_node_sum, grad_node_second], 0)
    new_grad_edges = edge_upstream + input_grad(d_edge16, weights[:width])
    new_grad_nodes = grad_nodes + input_grad(d_node, weights[4 * width:5 * width]) + input_grad(grad_send, weights[width:2 * width]) + input_grad(grad_recv, weights[2 * width:3 * width])
    return (new_grad_nodes, new_grad_edges, partial_value)

def reference(grid_latent, mesh_embed, mesh_edges, edge_geometry, edge_counts, edge_sources, edge_targets, halo_sources, mesh_sources, mesh_targets, grid_weight, geometry_weight, message_weight, mesh_update, mesh_output, processor, cotangent):
    senders, receivers = mesh_indices(halo_sources, mesh_sources, mesh_targets)
    layers = processor.shape[0]
    scale = 1.0 / math.sqrt(N_DP * MESH)

    def one_sample(inputs):
        grid_rows, upstream = inputs
        nodes = encode(grid_rows, mesh_embed, edge_geometry, edge_counts, edge_sources, edge_targets, grid_weight, geometry_weight, message_weight, mesh_update, mesh_output)
        edges = mesh_edges
        stored = []
        for layer_index in range(layers):
            new_nodes, new_edges, saved = layer_forward(nodes, edges, senders, receivers, processor[layer_index])
            stored.append((nodes, edges, saved))
            nodes, edges = (new_nodes, new_edges)
        result = nodes
        grad_nodes = upstream.astype(jnp.float32)
        grad_edges = jnp.zeros(edges.shape, jnp.float32)
        pieces = [None] * layers
        for layer_index in reversed(range(layers)):
            layer_nodes, layer_edges, saved = stored[layer_index]
            grad_nodes, grad_edges, partial_value = layer_backward(layer_nodes, layer_edges, senders, receivers, processor[layer_index], saved, grad_nodes, grad_edges)
            pieces[layer_index] = partial_value * scale
        return (result, grad_nodes.astype(jnp.bfloat16), jnp.stack(pieces))
    results, node_grads, partials = lax.map(one_sample, (grid_latent, cotangent))
    gradients = lax.optimization_barrier(jnp.sum(partials, axis=0)).astype(jnp.bfloat16)
    return (results, node_grads, gradients)
```

```python
import functools
import math

import jax
import jax.numpy as jnp
from jax import lax
from jax.experimental import pallas as pl
from jax.experimental.pallas import tpu as pltpu
from jax.sharding import PartitionSpec as P

EPSILON = 1e-05
F32, BF16 = jnp.float32, jnp.bfloat16
LANES = 128
TILE = 256
WE, WS, WR, E2, PV, PA, N2 = range(7)


def mm(left, right):
    return jnp.dot(left, right, preferred_element_type=F32)


def mm_tn(left, right):
    return lax.dot_general(left, right, (((0,), (0,)), ((), ())), preferred_element_type=F32)


def mm_nt(left, right):
    return lax.dot_general(left, right, (((1,), (1,)), ((), ())), preferred_element_type=F32)


def iota(shape, axis):
    return lax.broadcasted_iota(jnp.int32, shape, axis)


def hot(condition):
    return jnp.where(condition, 1.0, 0.0).astype(BF16)


def sigmoid(x):
    return 0.5 * jnp.tanh(0.5 * x) + 0.5


def normalize(y):
    center = jnp.mean(y, axis=-1, keepdims=True)
    shifted = y - center
    inverse = lax.rsqrt(jnp.mean(shifted * shifted, axis=-1, keepdims=True) + EPSILON)
    return shifted * inverse, inverse


def normalize_back(normed, inverse, upstream):
    first = jnp.mean(upstream, axis=-1, keepdims=True)
    second = jnp.mean(upstream * normed, axis=-1, keepdims=True)
    return inverse * (upstream - first - normed * second)


def rows(start, size):
    return pl.ds(pl.multiple_of(start * size, size), size)


def block(which, width):
    return pl.ds(which * width, width)


def column(row):
    return jnp.transpose(jnp.broadcast_to(row, (LANES, LANES)))


def row_hot(row, width):
    index = column(row)
    lane = iota((LANES, LANES), 1)
    return [hot(index == lane + k * LANES) for k in range(width // LANES)]


def pack(values, tiles):
    count, width = values.shape
    parts = width // LANES
    at, of = iota((count * parts, count), 0), iota((count * parts, count), 1)
    total = None
    for c in range(parts):
        piece = mm(hot(at == of * parts + c), values[:, c * LANES : (c + 1) * LANES])
        total = piece if total is None else total + piece
    tiles[...] = total.astype(BF16)


def unpack(tiles, width):
    parts = width // LANES
    total = tiles.shape[0]
    of, at = iota((total // parts, total), 0), iota((total // parts, total), 1)
    whole = tiles[...]
    return jnp.concatenate(
        [mm(hot(at == of * parts + c), whole).astype(BF16) for c in range(parts)], axis=1
    )


def messages_phase(grid, grid_weight, geometry, geometry_weight, counts, sources, out, proj):
    slots = sources.shape[1]
    peers = counts.shape[1]
    capacity = slots // peers
    grid_rows, width = grid.shape
    proj[...] = mm(grid[...], grid_weight[...]).astype(BF16)
    high = geometry_weight[...].astype(BF16)
    low = (geometry_weight[...] - high.astype(F32)).astype(BF16)
    count16 = jnp.broadcast_to(counts[...].astype(F32), (16, peers)).astype(BF16)

    def step(i, carry):
        at = rows(i, TILE)
        slot = i * TILE + iota((1, TILE), 1)
        owner = (i * TILE + iota((peers, TILE), 1)) // capacity
        limit = mm(count16, hot(owner == iota((peers, TILE), 0)))[:1]
        live = (slot % capacity).astype(F32) < limit
        index = jnp.where(live, sources[:, at], -1)
        shape = jnp.where(live, geometry[:, at].astype(F32), 0.0).astype(BF16)
        table = jnp.concatenate(
            [
                jnp.concatenate(row_hot(index[:, k : k + LANES], grid_rows), axis=1)
                for k in range(0, TILE, LANES)
            ],
            axis=0,
        )
        pre = mm(table, proj[...]) + mm_tn(shape, high) + mm_tn(shape, low)
        out[at, :] = (pre * sigmoid(pre)).astype(BF16)
        return carry

    lax.fori_loop(0, slots // TILE, step, 0)


def tables_phase(senders, receivers, gather, scatter, extended):
    edges = senders.shape[1]
    nodes = gather.shape[1] - extended

    def step(i, carry):
        at = rows(i, LANES)
        send, recv = senders[:, at], receivers[:, at]
        gather[at, :extended] = jnp.concatenate(row_hot(send, extended), axis=1)
        gather[at, extended:] = jnp.concatenate(row_hot(recv, nodes), axis=1)
        scatter[:extended, at] = hot(iota((extended, LANES), 0) == send)
        scatter[extended:, at] = hot(iota((nodes, LANES), 0) == recv)
        return carry

    lax.fori_loop(0, edges // LANES, step, 0)


def halo_send(nodes, halo, tiles):
    picked = jnp.concatenate(
        [
            jnp.concatenate(row_hot(halo[:, k : k + LANES], nodes.shape[0]), axis=1)
            for k in range(0, halo.shape[1], LANES)
        ],
        axis=0,
    )
    pack(mm(picked, nodes).astype(BF16), tiles)


def start_phase(arrived, targets, embed, message_weight, update, output, nodes, total):
    slots = targets.shape[1]
    count, width = embed.shape
    total[...] = jnp.zeros_like(total)

    def step(i, carry):
        at = rows(i, 2 * TILE)
        total[...] += mm(hot(iota((count, 2 * TILE), 0) == targets[:, at]), arrived[at, :])
        return carry

    lax.fori_loop(0, slots // (2 * TILE), step, 0)
    aggregate = mm(total[...].astype(BF16), message_weight[...]).astype(BF16)
    pre = mm(embed[...], update[:width]) + mm(aggregate, update[width:])
    normed, _ = normalize(mm((pre * sigmoid(pre)).astype(BF16), output[...]))
    nodes[...] = (embed[...].astype(F32) + normed).astype(BF16)


def forward_phase(weights, nodes, incoming, edges, gather, scatter, saved, new_nodes, proj, total):
    count, width = nodes.shape
    w = lambda which: weights[block(which, width), :]
    extended = gather.shape[1] - count
    proj[:count] = mm(nodes[...], w(WS)).astype(BF16)
    proj[count:extended] = mm(unpack(incoming, width), w(WS)).astype(BF16)
    proj[extended:] = mm(nodes[...], w(WR)).astype(BF16)
    total[...] = jnp.zeros_like(total)

    def step(i, carry):
        at = rows(i, TILE)
        x = edges[at, :]
        pre = mm(x, w(WE)) + mm(gather[at, :], proj[...])
        s = sigmoid(pre)
        act = pre * s
        hid = act.astype(BF16)
        saved["hid"][at, :] = hid
        saved["slope"][at, :] = (s + act * (1.0 - s)).astype(BF16)
        normed, inverse = normalize(mm(hid, w(E2)))
        saved["normed"][at, :] = normed.astype(BF16)
        saved["inverse"][at, :] = jnp.broadcast_to(inverse, (TILE, LANES))
        new = (x.astype(F32) + normed).astype(BF16)
        if saved["edges"] is not None:
            saved["edges"][at, :] = new
        total[...] += mm(scatter[extended:, at], new)
        return carry

    lax.fori_loop(0, edges.shape[0] // TILE, step, 0)
    summed = total[...].astype(BF16)
    pre = mm(nodes[...], w(PV)) + mm(summed, w(PA))
    s = sigmoid(pre)
    act = pre * s
    hid = act.astype(BF16)
    normed, inverse = normalize(mm(hid, w(N2)))
    new_nodes[...] = (nodes[...].astype(F32) + normed).astype(BF16)
    saved["summed"][...] = summed
    saved["node_hid"][...] = hid
    saved["node_slope"][...] = s + act * (1.0 - s)
    saved["node_normed"][...] = normed
    saved["node_inverse"][...] = jnp.broadcast_to(inverse, (count, LANES))


def backward_phase(
    scale, weights, nodes, edges, gather, scatter, saved, grad_nodes, grad_edges, first, last,
    grads, tiles, send, proj, total, acc,
):
    count, width = nodes.shape
    w = lambda which: weights[block(which, width), :]
    extended = gather.shape[1] - count
    upstream = grad_nodes[...]
    q = normalize_back(saved["node_normed"][...], saved["node_inverse"][:, :1], upstream)
    q = q.astype(BF16)

    def put(which, value):
        grads[block(which, width), :] = (value * scale).astype(BF16)

    put(N2, mm_tn(saved["node_hid"][...], q))
    d_node = (mm_nt(q, w(N2)) * saved["node_slope"][...]).astype(BF16)
    put(PV, mm_tn(nodes[...], d_node))
    put(PA, mm_tn(saved["summed"][...], d_node))
    proj[extended:] = mm_nt(d_node, w(PA)).astype(BF16)
    grad_nodes[...] = upstream + mm_nt(d_node, w(PV))
    total[...] = jnp.zeros_like(total)
    acc[...] = jnp.zeros_like(acc)

    def step(i, carry):
        at = rows(i, TILE)
        up = mm(gather[at, extended:], proj[extended:])
        if not first:
            up = up + grad_edges[at, :]
        q = normalize_back(saved["normed"][at, :].astype(F32), saved["inverse"][at, :1], up)
        q = q.astype(BF16)
        acc[width:] += mm_tn(saved["hid"][at, :], q)
        d = (mm_nt(q, w(E2)) * saved["slope"][at, :].astype(F32)).astype(BF16)
        acc[:width] += mm_tn(edges[at, :], d)
        total[...] += mm(scatter[:, at], d)
        if not last:
            grad_edges[at, :] = up + mm_nt(d, w(WE))
        return carry

    lax.fori_loop(0, edges.shape[0] // TILE, step, 0)
    put(WE, acc[:width])
    put(E2, acc[width:])
    pack(total[count:extended].astype(BF16), tiles)
    send[...] = total[:count]
    recv = total[extended:].astype(BF16)
    put(WR, mm_tn(nodes[...], recv))
    grad_nodes[...] += mm_nt(recv, w(WR))


def finish_phase(scale, weights, nodes, returned, halo, send, grad_nodes, put):
    count, width = nodes.shape
    back = hot(iota((count, halo.shape[1]), 0) == halo[...])
    total = (send[...] + mm(back, unpack(returned, width))).astype(BF16)
    put((mm_tn(nodes[...], total) * scale).astype(BF16))
    grad_nodes[...] += mm_nt(total, weights[block(WS, width), :])


SAVED = ("hid", "slope", "normed", "inverse", "edges", "summed", "node_hid", "node_slope", "node_normed", "node_inverse")


def saved_shapes(edges, nodes, width, with_edges):
    shapes = {
        "hid": ((edges, width), BF16),
        "slope": ((edges, width), BF16),
        "normed": ((edges, width), BF16),
        "inverse": ((edges, LANES), F32),
        "edges": ((edges, width), BF16),
        "summed": ((nodes, width), BF16),
        "node_hid": ((nodes, width), BF16),
        "node_slope": ((nodes, width), F32),
        "node_normed": ((nodes, width), F32),
        "node_inverse": ((nodes, LANES), F32),
    }
    return [shapes[name] for name in SAVED if with_edges or name != "edges"]


def saved_refs(refs, with_edges):
    names = [name for name in SAVED if with_edges or name != "edges"]
    found = dict(zip(names, refs))
    found.setdefault("edges", None)
    return found


def call(kernel, args, outs, scratch=(), aliases=None):
    vmem = pl.BlockSpec(memory_space=pltpu.VMEM)
    return pl.pallas_call(
        kernel,
        out_shape=[jax.ShapeDtypeStruct(*out) for out in outs],
        in_specs=[vmem] * len(args),
        out_specs=[vmem] * len(outs),
        scratch_shapes=[pltpu.VMEM(*s) for s in scratch],
        input_output_aliases=aliases or {},
    )(*args)


def on_device(
    grid_latent,
    mesh_embed,
    mesh_edges,
    edge_geometry,
    edge_counts,
    edge_sources,
    edge_targets,
    halo_sources,
    mesh_sources,
    mesh_targets,
    grid_weight,
    geometry_weight,
    message_weight,
    mesh_update,
    mesh_output,
    processor,
    cotangent,
):
    count, width = mesh_embed.shape
    edges = mesh_edges.shape[0]
    slots = edge_sources.shape[1]
    halo = halo_sources.shape[1]
    peers = lax.axis_size("graph")
    grid_rows = grid_latent.shape[1]
    extended = count + halo
    table = extended + count
    parts = width // LANES
    tiles = (halo * parts, LANES)
    scale = 1.0 / math.sqrt(lax.axis_size("dp") * peers * count)
    exchange = lambda values: lax.all_to_all(
        values.reshape(peers, -1, values.shape[-1]), "graph", split_axis=0, concat_axis=0, tiled=True
    ).reshape(values.shape)

    (messages,) = call(
        lambda *refs: messages_phase(*refs),
        (grid_latent[0], grid_weight, edge_geometry[0], geometry_weight, edge_counts, edge_sources),
        [((slots, width), BF16)],
        [((grid_rows, width), BF16)],
    )
    arrived = exchange(messages)
    gather, scatter = call(
        lambda *refs: tables_phase(*refs, extended),
        (mesh_sources, mesh_targets),
        [((edges, table), BF16), ((table, edges), BF16)],
    )

    def begin(arrived, targets, embed, message_weight, update, output, halo, nodes, out, total):
        start_phase(arrived, targets, embed, message_weight, update, output, nodes, total)
        halo_send(nodes[...], halo, out)

    nodes0, out = call(
        begin,
        (arrived, edge_targets, mesh_embed, message_weight, mesh_update, mesh_output, halo_sources),
        [((count, width), BF16), (tiles, BF16)],
        [((count, width), F32)],
    )
    incoming = exchange(out)
    wide = [((table, width), BF16), ((count, width), F32)]

    def layer0(weights, nodes, incoming, edges, gather, scatter, halo, new_nodes, out, *rest):
        saved = saved_refs(rest[:-2], True)
        forward_phase(weights, nodes, incoming, edges, gather, scatter, saved, new_nodes, *rest[-2:])
        halo_send(new_nodes[...], halo, out)

    nodes1, out, *saved0 = call(
        layer0,
        (processor[0], nodes0, incoming, mesh_edges, gather, scatter, halo_sources),
        [((count, width), BF16), (tiles, BF16), *saved_shapes(edges, count, width, True)],
        wide,
    )
    incoming = exchange(out)
    edges1 = saved0[SAVED.index("edges")]
    grads_shape = ((7 * width, width), BF16)
    work = [
        ((table, width), BF16),
        ((table, width), F32),
        ((2 * width, width), F32),
    ]
    n_saved = len(SAVED) - 1

    def layer1(
        weights, nodes, incoming, edges, gather, scatter, cot, new_nodes, grads, tiles, send,
        grad_nodes, grad_edges, *rest,
    ):
        saved = saved_refs(rest[:n_saved], False)
        total_f, proj, total, acc = rest[n_saved:]
        forward_phase(weights, nodes, incoming, edges, gather, scatter, saved, new_nodes, proj, total_f)
        grad_nodes[...] = cot[...].astype(F32)
        grads[block(WS, width), :] = jnp.zeros((width, width), BF16)
        backward_phase(
            scale, weights, nodes, edges, gather, scatter, saved, grad_nodes, grad_edges, True, False,
            grads, tiles, send, proj, total, acc,
        )

    nodes2, grads1, back, send, grad_nodes, grad_edges = call(
        layer1,
        (processor[1], nodes1, incoming, edges1, gather, scatter, cotangent[0]),
        [
            ((count, width), BF16),
            grads_shape,
            (tiles, BF16),
            ((count, width), F32),
            ((count, width), F32),
            ((edges, width), F32),
        ],
        [*saved_shapes(edges, count, width, False), ((count, width), F32), *work],
    )
    returned = exchange(back)

    def middle(
        weights1, nodes1, returned, halo, send1, gn, weights, nodes, edges, gather, scatter, ge, *rest
    ):
        saved = saved_refs(rest[: len(SAVED)], True)
        grads, tiles, send, grad_nodes, proj, total, acc = rest[len(SAVED) :]
        grad_nodes[...] = gn[...]

        def put(value):
            grads[7 * width :, :] = value

        finish_phase(scale, weights1, nodes1, returned, halo, send1, grad_nodes, put)
        backward_phase(
            scale, weights, nodes, edges, gather, scatter, saved, grad_nodes, ge, False, True,
            grads, tiles, send, proj, total, acc,
        )

    grads0, back, send, grad_nodes = call(
        middle,
        (
            processor[1], nodes1, returned, halo_sources, send, grad_nodes, processor[0], nodes0,
            mesh_edges, gather, scatter, grad_edges, *saved0,
        ),
        [
            ((8 * width, width), BF16),
            (tiles, BF16),
            ((count, width), F32),
            ((count, width), F32),
        ],
        work,
    )
    returned = exchange(back)

    def end(weights, nodes, returned, halo, send, gn, last_grad, result, total):
        total[...] = gn[...]

        def put(value):
            last_grad[...] = value

        finish_phase(scale, weights, nodes, returned, halo, send, total, put)
        result[...] = total[...].astype(BF16)

    last0, result = call(
        end,
        (processor[0], nodes0, returned, halo_sources, send, grad_nodes),
        [((width, width), BF16), ((count, width), BF16)],
        [((count, width), F32)],
    )
    whole1 = lax.psum(grads1, ("graph", "dp"))
    grads0 = lax.dynamic_update_slice(grads0, last0, (width, 0))
    grads0, whole1 = lax.optimization_barrier((grads0, whole1))
    whole0 = lax.psum(grads0, ("graph", "dp"))
    whole1 = lax.dynamic_update_slice(whole1, whole0[7 * width :], (width, 0))
    gradients = jnp.stack([whole0[: 7 * width], whole1])
    return nodes2[None], result[None], gradients


def solution(mesh):
    in_specs = (
        P("dp", "graph", None),
        P("graph", None),
        P("graph", None),
        P("graph", None, None),
        P("graph", None),
        P("graph", None),
        P("graph", None),
        P("graph", None),
        P("graph", None),
        P("graph", None),
        P(),
        P(),
        P(),
        P(),
        P(),
        P(),
        P("dp", "graph", None),
    )
    out_specs = (P("dp", "graph", None), P("dp", "graph", None), P())
    return jax.shard_map(
        on_device, mesh=mesh, in_specs=in_specs, out_specs=out_specs, check_vma=False
    )
```

```python
import functools
import math

import jax
import jax.numpy as jnp
from jax import lax
from jax.experimental import pallas as pl
from jax.experimental.pallas import tpu as pltpu
from jax.sharding import PartitionSpec as P

EPSILON = 1e-05
F32, BF16 = jnp.float32, jnp.bfloat16
LANES = 128
TILE = 256
WE, WS, WR, E2, PV, PA, N2 = range(7)


def mm(left, right):
    return jnp.dot(left, right, preferred_element_type=F32)


def mm_tn(left, right):
    return lax.dot_general(left, right, (((0,), (0,)), ((), ())), preferred_element_type=F32)


def mm_nt(left, right):
    return lax.dot_general(left, right, (((1,), (1,)), ((), ())), preferred_element_type=F32)


def iota(shape, axis):
    return lax.broadcasted_iota(jnp.int32, shape, axis)


def hot(condition):
    return jnp.where(condition, 1.0, 0.0).astype(BF16)


def sigmoid(x):
    return 0.5 * jnp.tanh(0.5 * x) + 0.5


def normalize(y):
    center = jnp.mean(y, axis=-1, keepdims=True)
    shifted = y - center
    inverse = lax.rsqrt(jnp.mean(shifted * shifted, axis=-1, keepdims=True) + EPSILON)
    return shifted * inverse, inverse


def normalize_back(normed, inverse, upstream):
    first = jnp.mean(upstream, axis=-1, keepdims=True)
    second = jnp.mean(upstream * normed, axis=-1, keepdims=True)
    return inverse * (upstream - first - normed * second)


def rows(start, size):
    return pl.ds(pl.multiple_of(start * size, size), size)


def block(which, width):
    return pl.ds(which * width, width)


def column(row):
    return jnp.transpose(jnp.broadcast_to(row, (LANES, LANES)))


def row_hot(row, width):
    index = column(row)
    lane = iota((LANES, LANES), 1)
    return [hot(index == lane + k * LANES) for k in range(width // LANES)]


def pack(values, tiles):
    count, width = values.shape
    parts = width // LANES
    at, of = iota((count * parts, count), 0), iota((count * parts, count), 1)
    total = None
    for c in range(parts):
        piece = mm(hot(at == of * parts + c), values[:, c * LANES : (c + 1) * LANES])
        total = piece if total is None else total + piece
    tiles[...] = total.astype(BF16)


def unpack(tiles, width):
    parts = width // LANES
    total = tiles.shape[0]
    of, at = iota((total // parts, total), 0), iota((total // parts, total), 1)
    whole = tiles[...]
    return jnp.concatenate(
        [mm(hot(at == of * parts + c), whole).astype(BF16) for c in range(parts)], axis=1
    )


def messages_phase(grid, grid_weight, geometry, geometry_weight, counts, sources, out, proj):
    slots = sources.shape[1]
    peers = counts.shape[1]
    capacity = slots // peers
    grid_rows, width = grid.shape
    proj[...] = mm(grid[...], grid_weight[...]).astype(BF16)
    high = geometry_weight[...].astype(BF16)
    low = (geometry_weight[...] - high.astype(F32)).astype(BF16)
    count16 = jnp.broadcast_to(counts[...].astype(F32), (16, peers)).astype(BF16)

    def step(i, carry):
        at = rows(i, TILE)
        slot = i * TILE + iota((1, TILE), 1)
        owner = (i * TILE + iota((peers, TILE), 1)) // capacity
        limit = mm(count16, hot(owner == iota((peers, TILE), 0)))[:1]
        live = (slot % capacity).astype(F32) < limit
        index = jnp.where(live, sources[:, at], -1)
        shape = jnp.where(live, geometry[:, at].astype(F32), 0.0).astype(BF16)
        table = jnp.concatenate(
            [
                jnp.concatenate(row_hot(index[:, k : k + LANES], grid_rows), axis=1)
                for k in range(0, TILE, LANES)
            ],
            axis=0,
        )
        pre = mm(table, proj[...]) + mm_tn(shape, high) + mm_tn(shape, low)
        out[at, :] = (pre * sigmoid(pre)).astype(BF16)
        return carry

    lax.fori_loop(0, slots // TILE, step, 0)


def tables_phase(senders, receivers, gather, scatter, extended):
    edges = senders.shape[1]
    nodes = gather.shape[1] - extended

    def step(i, carry):
        at = rows(i, LANES)
        send, recv = senders[:, at], receivers[:, at]
        gather[at, :extended] = jnp.concatenate(row_hot(send, extended), axis=1)
        gather[at, extended:] = jnp.concatenate(row_hot(recv, nodes), axis=1)
        scatter[:extended, at] = hot(iota((extended, LANES), 0) == send)
        scatter[extended:, at] = hot(iota((nodes, LANES), 0) == recv)
        return carry

    lax.fori_loop(0, edges // LANES, step, 0)


def halo_send(nodes, halo, tiles):
    picked = jnp.concatenate(
        [
            jnp.concatenate(row_hot(halo[:, k : k + LANES], nodes.shape[0]), axis=1)
            for k in range(0, halo.shape[1], LANES)
        ],
        axis=0,
    )
    pack(mm(picked, nodes).astype(BF16), tiles)


def start_phase(arrived, targets, embed, message_weight, update, output, nodes, total):
    slots = targets.shape[1]
    count, width = embed.shape
    total[...] = jnp.zeros_like(total)

    def step(i, carry):
        at = rows(i, 2 * TILE)
        total[...] += mm(hot(iota((count, 2 * TILE), 0) == targets[:, at]), arrived[at, :])
        return carry

    lax.fori_loop(0, slots // (2 * TILE), step, 0)
    aggregate = mm(total[...].astype(BF16), message_weight[...]).astype(BF16)
    pre = mm(embed[...], update[:width]) + mm(aggregate, update[width:])
    normed, _ = normalize(mm((pre * sigmoid(pre)).astype(BF16), output[...]))
    nodes[...] = (embed[...].astype(F32) + normed).astype(BF16)


def forward_phase(weights, nodes, incoming, edges, gather, scatter, saved, new_nodes, proj, total):
    count, width = nodes.shape
    w = lambda which: weights[block(which, width), :]
    extended = gather.shape[1] - count
    proj[:count] = mm(nodes[...], w(WS)).astype(BF16)
    proj[count:extended] = mm(unpack(incoming, width), w(WS)).astype(BF16)
    proj[extended:] = mm(nodes[...], w(WR)).astype(BF16)
    total[...] = jnp.zeros_like(total)

    def step(i, carry):
        at = rows(i, TILE)
        x = edges[at, :]
        pre = mm(x, w(WE)) + mm(gather[at, :], proj[...])
        s = sigmoid(pre)
        act = pre * s
        hid = act.astype(BF16)
        saved["hid"][at, :] = hid
        saved["slope"][at, :] = (s + act * (1.0 - s)).astype(BF16)
        normed, inverse = normalize(mm(hid, w(E2)))
        saved["normed"][at, :] = normed.astype(BF16)
        saved["inverse"][at, :] = jnp.broadcast_to(inverse, (TILE, LANES))
        new = (x.astype(F32) + normed).astype(BF16)
        if saved["edges"] is not None:
            saved["edges"][at, :] = new
        total[...] += mm(scatter[extended:, at], new)
        return carry

    lax.fori_loop(0, edges.shape[0] // TILE, step, 0)
    summed = total[...].astype(BF16)
    pre = mm(nodes[...], w(PV)) + mm(summed, w(PA))
    s = sigmoid(pre)
    act = pre * s
    hid = act.astype(BF16)
    normed, inverse = normalize(mm(hid, w(N2)))
    new_nodes[...] = (nodes[...].astype(F32) + normed).astype(BF16)
    saved["summed"][...] = summed
    saved["node_hid"][...] = hid
    saved["node_slope"][...] = s + act * (1.0 - s)
    saved["node_normed"][...] = normed
    saved["node_inverse"][...] = jnp.broadcast_to(inverse, (count, LANES))


def backward_phase(
    scale, weights, nodes, edges, gather, scatter, saved, grad_nodes, grad_edges, first, last,
    grads, tiles, send, proj, total, acc,
):
    count, width = nodes.shape
    w = lambda which: weights[block(which, width), :]
    extended = gather.shape[1] - count
    upstream = grad_nodes[...]
    q = normalize_back(saved["node_normed"][...], saved["node_inverse"][:, :1], upstream)
    q = q.astype(BF16)

    def put(which, value):
        grads[block(which, width), :] = (value * scale).astype(BF16)

    put(N2, mm_tn(saved["node_hid"][...], q))
    d_node = (mm_nt(q, w(N2)) * saved["node_slope"][...]).astype(BF16)
    put(PV, mm_tn(nodes[...], d_node))
    put(PA, mm_tn(saved["summed"][...], d_node))
    proj[extended:] = mm_nt(d_node, w(PA)).astype(BF16)
    grad_nodes[...] = upstream + mm_nt(d_node, w(PV))
    total[...] = jnp.zeros_like(total)
    acc[...] = jnp.zeros_like(acc)

    def step(i, carry):
        at = rows(i, TILE)
        up = mm(gather[at, extended:], proj[extended:])
        if not first:
            up = up + grad_edges[at, :]
        q = normalize_back(saved["normed"][at, :].astype(F32), saved["inverse"][at, :1], up)
        q = q.astype(BF16)
        acc[width:] += mm_tn(saved["hid"][at, :], q)
        d = (mm_nt(q, w(E2)) * saved["slope"][at, :].astype(F32)).astype(BF16)
        acc[:width] += mm_tn(edges[at, :], d)
        total[...] += mm(scatter[:, at], d)
        if not last:
            grad_edges[at, :] = up + mm_nt(d, w(WE))
        return carry

    lax.fori_loop(0, edges.shape[0] // TILE, step, 0)
    put(WE, acc[:width])
    put(E2, acc[width:])
    pack(total[count:extended].astype(BF16), tiles)
    send[...] = total[:count]
    recv = total[extended:].astype(BF16)
    put(WR, mm_tn(nodes[...], recv))
    grad_nodes[...] += mm_nt(recv, w(WR))


def finish_phase(scale, weights, nodes, returned, halo, send, grad_nodes, put):
    count, width = nodes.shape
    back = hot(iota((count, halo.shape[1]), 0) == halo[...])
    total = (send[...] + mm(back, unpack(returned, width))).astype(BF16)
    put((mm_tn(nodes[...], total) * scale).astype(BF16))
    grad_nodes[...] += mm_nt(total, weights[block(WS, width), :])


class Reducer:
    def __init__(self, source, result, refs):
        (self.half_in, self.half, self.quarter_in, self.quarter, self.tile_in, self.sent, self.got) = refs
        self.source, self.result = source, result
        graph, dp = lax.axis_index("graph"), lax.axis_index("dp")
        self.core = lax.rem(graph, 2)
        self.place = [lax.rem(graph // 2, 4), graph // 8, dp]

    def device(self, core, place):
        return (place[1] * 8 + place[0] * 2 + core, place[2])

    def partner(self):
        return self.device(1 - self.core, self.place)

    def along(self, axis, k):
        place = list(self.place)
        place[axis] = lax.rem(place[axis] + k, 4)
        return place[axis], self.device(self.core, place)

    def over(self, axis, k):
        first, second = [a for a in range(3) if a != axis]
        where = lax.rem(self.place[first] * 4 + self.place[second] + k, 16)
        place = list(self.place)
        place[first], place[second] = where // 4, lax.rem(where, 4)
        return where, self.device(self.core, place)

    def enter(self):
        barrier = pltpu.get_barrier_semaphore()
        pl.semaphore_signal(barrier, inc=1, device_id=self.partner(), device_id_type=pl.DeviceIdType.MESH)
        for axis in range(3):

            def greet(k, carry):
                _, device = self.over(axis, k)
                pl.semaphore_signal(barrier, inc=1, device_id=device, device_id_type=pl.DeviceIdType.MESH)
                return carry

            lax.fori_loop(1, 16, greet, 0)
        pl.semaphore_wait(barrier, 46)

    def send(self, b, stage, source, target, device):
        pltpu.make_async_remote_copy(
            src_ref=source,
            dst_ref=target,
            send_sem=self.sent.at[b, stage],
            recv_sem=self.got.at[b, stage],
            device_id=device,
            device_id_type=pl.DeviceIdType.MESH,
        ).start()

    def wait(self, semaphores, b, stage):
        sizes = (
            self.half_in.at[b], self.quarter_in.at[b], self.tile_in.at[b],
            self.tile_in.at[b], self.quarter_in.at[b], self.half_in.at[b],
        )
        pltpu.make_async_copy(sizes[stage], sizes[stage], semaphores.at[b, stage]).wait()

    def spot(self, where):
        at = pl.multiple_of((where // 4) * 16, 16)
        lane = pl.multiple_of(lax.rem(where, 4) * LANES, LANES)
        return at, lane

    def begin(self, b):
        start = pl.multiple_of((1 - self.core) * 256, 256)
        self.send(b, 0, self.source(b).at[pl.ds(start, 256)], self.half_in.at[b], self.partner())

    def step1(self, b):
        self.wait(self.got, b, 0)
        start = pl.multiple_of(self.core * 256, 256)
        mine = self.source(b)[pl.ds(start, 256), :]
        self.half[b] = (mine.astype(F32) + self.half_in[b].astype(F32)).astype(BF16)
        for k in range(1, 4):
            at, device = self.along(b % 3, k)
            at = pl.multiple_of(at * 64, 64)
            self.send(b, 1, self.half.at[b, pl.ds(at, 64)], self.quarter_in.at[b, k - 1], device)

    def step2(self, b):
        self.wait(self.got, b, 1)
        at = pl.multiple_of(self.place[b % 3] * 64, 64)
        total = self.half[b, pl.ds(at, 64), :].astype(F32)
        for k in range(3):
            total = total + self.quarter_in[b, k].astype(F32)
        self.quarter[b] = total.astype(BF16)

        def one(k, carry):
            where, device = self.over(b % 3, k)
            at, lane = self.spot(where)
            self.send(b, 2, self.quarter.at[b, pl.ds(at, 16), pl.ds(lane, LANES)], self.tile_in.at[b, k - 1], device)
            return carry

        lax.fori_loop(1, 16, one, 0)

    def step3(self, b):
        self.wait(self.got, b, 2)
        where, _ = self.over(b % 3, 0)
        at, lane = self.spot(where)
        total = self.quarter[b, pl.ds(at, 16), pl.ds(lane, LANES)].astype(F32)
        total = total + jnp.sum(self.tile_in[b].astype(F32), axis=0)
        base = self.core * 256 + self.place[b % 3] * 64
        mine = self.result.at[b, pl.ds(pl.multiple_of(base + at, 16), 16), pl.ds(lane, LANES)]
        mine[...] = total.astype(BF16)

        def one(k, carry):
            _, device = self.over(b % 3, k)
            self.send(b, 3, mine, mine, device)
            return carry

        lax.fori_loop(1, 16, one, 0)

    def step4(self, b):
        self.wait(self.got, b, 3)
        base = pl.multiple_of(self.core * 256 + self.place[b % 3] * 64, 64)
        mine = self.result.at[b, pl.ds(base, 64)]
        for k in range(1, 4):
            self.send(b, 4, mine, mine, self.along(b % 3, k)[1])

    def step5(self, b):
        self.wait(self.got, b, 4)
        mine = self.result.at[b, pl.ds(pl.multiple_of(self.core * 256, 256), 256)]
        self.send(b, 5, mine, mine, self.partner())

    def step6(self, b):
        self.wait(self.got, b, 5)

    def leave(self, b):
        for stage in range(6):
            self.wait(self.sent, b, stage)


def reducer_scratch(blocks):
    return [
        pltpu.VMEM((blocks, 256, 512), BF16),
        pltpu.VMEM((blocks, 256, 512), BF16),
        pltpu.VMEM((blocks, 3, 64, 512), BF16),
        pltpu.VMEM((blocks, 64, 512), BF16),
        pltpu.VMEM((blocks, 15, 16, LANES), BF16),
        pltpu.SemaphoreType.DMA((blocks, 6)),
        pltpu.SemaphoreType.DMA((blocks, 6)),
    ]


def reduce_phase(grads1, grads0, last0, result, *refs):
    def source(b):
        layer, which = divmod(b, 7)
        if layer == 0:
            return last0 if which == WS else grads0.at[block(which, 512)]
        return grads0.at[block(7, 512)] if which == WS else grads1.at[block(which, 512)]

    reducer = Reducer(source, result, refs)
    reducer.enter()
    blocks = range(14)
    steps = (
        reducer.begin, reducer.step1, reducer.step2, reducer.step3, reducer.step4, reducer.step5,
        reducer.step6, reducer.leave,
    )
    for step in steps:
        for b in blocks:
            step(b)


SAVED = ("hid", "slope", "normed", "inverse", "edges", "summed", "node_hid", "node_slope", "node_normed", "node_inverse")


def saved_shapes(edges, nodes, width, with_edges):
    shapes = {
        "hid": ((edges, width), BF16),
        "slope": ((edges, width), BF16),
        "normed": ((edges, width), BF16),
        "inverse": ((edges, LANES), F32),
        "edges": ((edges, width), BF16),
        "summed": ((nodes, width), BF16),
        "node_hid": ((nodes, width), BF16),
        "node_slope": ((nodes, width), F32),
        "node_normed": ((nodes, width), F32),
        "node_inverse": ((nodes, LANES), F32),
    }
    return [shapes[name] for name in SAVED if with_edges or name != "edges"]


def saved_refs(refs, with_edges):
    names = [name for name in SAVED if with_edges or name != "edges"]
    found = dict(zip(names, refs))
    found.setdefault("edges", None)
    return found


def call(kernel, args, outs, scratch=(), aliases=None):
    vmem = pl.BlockSpec(memory_space=pltpu.VMEM)
    return pl.pallas_call(
        kernel,
        out_shape=[jax.ShapeDtypeStruct(*out) for out in outs],
        in_specs=[vmem] * len(args),
        out_specs=[vmem] * len(outs),
        scratch_shapes=[pltpu.VMEM(*s) for s in scratch],
        input_output_aliases=aliases or {},
    )(*args)


def on_device(
    grid_latent,
    mesh_embed,
    mesh_edges,
    edge_geometry,
    edge_counts,
    edge_sources,
    edge_targets,
    halo_sources,
    mesh_sources,
    mesh_targets,
    grid_weight,
    geometry_weight,
    message_weight,
    mesh_update,
    mesh_output,
    processor,
    cotangent,
):
    count, width = mesh_embed.shape
    edges = mesh_edges.shape[0]
    slots = edge_sources.shape[1]
    halo = halo_sources.shape[1]
    peers = lax.axis_size("graph")
    grid_rows = grid_latent.shape[1]
    extended = count + halo
    table = extended + count
    parts = width // LANES
    tiles = (halo * parts, LANES)
    scale = 1.0 / math.sqrt(lax.axis_size("dp") * peers * count)
    exchange = lambda values: lax.all_to_all(
        values.reshape(peers, -1, values.shape[-1]), "graph", split_axis=0, concat_axis=0, tiled=True
    ).reshape(values.shape)

    (messages,) = call(
        lambda *refs: messages_phase(*refs),
        (grid_latent[0], grid_weight, edge_geometry[0], geometry_weight, edge_counts, edge_sources),
        [((slots, width), BF16)],
        [((grid_rows, width), BF16)],
    )
    arrived = exchange(messages)
    gather, scatter = call(
        lambda *refs: tables_phase(*refs, extended),
        (mesh_sources, mesh_targets),
        [((edges, table), BF16), ((table, edges), BF16)],
    )

    def begin(arrived, targets, embed, message_weight, update, output, halo, nodes, out, total):
        start_phase(arrived, targets, embed, message_weight, update, output, nodes, total)
        halo_send(nodes[...], halo, out)

    nodes0, out = call(
        begin,
        (arrived, edge_targets, mesh_embed, message_weight, mesh_update, mesh_output, halo_sources),
        [((count, width), BF16), (tiles, BF16)],
        [((count, width), F32)],
    )
    incoming = exchange(out)
    wide = [((table, width), BF16), ((count, width), F32)]

    def layer0(weights, nodes, incoming, edges, gather, scatter, halo, new_nodes, out, *rest):
        saved = saved_refs(rest[:-2], True)
        forward_phase(weights, nodes, incoming, edges, gather, scatter, saved, new_nodes, *rest[-2:])
        halo_send(new_nodes[...], halo, out)

    nodes1, out, *saved0 = call(
        layer0,
        (processor[0], nodes0, incoming, mesh_edges, gather, scatter, halo_sources),
        [((count, width), BF16), (tiles, BF16), *saved_shapes(edges, count, width, True)],
        wide,
    )
    incoming = exchange(out)
    edges1 = saved0[SAVED.index("edges")]
    grads_shape = ((7 * width, width), BF16)
    work = [
        ((table, width), BF16),
        ((table, width), F32),
        ((2 * width, width), F32),
    ]
    n_saved = len(SAVED) - 1

    def layer1(
        weights, nodes, incoming, edges, gather, scatter, cot, new_nodes, grads, tiles, send,
        grad_nodes, grad_edges, *rest,
    ):
        saved = saved_refs(rest[:n_saved], False)
        total_f, proj, total, acc = rest[n_saved:]
        forward_phase(weights, nodes, incoming, edges, gather, scatter, saved, new_nodes, proj, total_f)
        grad_nodes[...] = cot[...].astype(F32)
        grads[block(WS, width), :] = jnp.zeros((width, width), BF16)
        backward_phase(
            scale, weights, nodes, edges, gather, scatter, saved, grad_nodes, grad_edges, True, False,
            grads, tiles, send, proj, total, acc,
        )

    nodes2, grads1, back, send, grad_nodes, grad_edges = call(
        layer1,
        (processor[1], nodes1, incoming, edges1, gather, scatter, cotangent[0]),
        [
            ((count, width), BF16),
            grads_shape,
            (tiles, BF16),
            ((count, width), F32),
            ((count, width), F32),
            ((edges, width), F32),
        ],
        [*saved_shapes(edges, count, width, False), ((count, width), F32), *work],
    )
    returned = exchange(back)

    def middle(
        weights1, nodes1, returned, halo, send1, gn, weights, nodes, edges, gather, scatter, ge, *rest
    ):
        saved = saved_refs(rest[: len(SAVED)], True)
        grads, tiles, send, grad_nodes, proj, total, acc = rest[len(SAVED) :]
        grad_nodes[...] = gn[...]

        def put(value):
            grads[7 * width :, :] = value

        finish_phase(scale, weights1, nodes1, returned, halo, send1, grad_nodes, put)
        backward_phase(
            scale, weights, nodes, edges, gather, scatter, saved, grad_nodes, ge, False, True,
            grads, tiles, send, proj, total, acc,
        )

    grads0, back, send, grad_nodes = call(
        middle,
        (
            processor[1], nodes1, returned, halo_sources, send, grad_nodes, processor[0], nodes0,
            mesh_edges, gather, scatter, grad_edges, *saved0,
        ),
        [
            ((8 * width, width), BF16),
            (tiles, BF16),
            ((count, width), F32),
            ((count, width), F32),
        ],
        work,
    )
    returned = exchange(back)

    def end(weights, nodes, returned, halo, send, gn, last_grad, result, total):
        total[...] = gn[...]

        def put(value):
            last_grad[...] = value

        finish_phase(scale, weights, nodes, returned, halo, send, total, put)
        result[...] = total[...].astype(BF16)

    last0, result = call(
        end,
        (processor[0], nodes0, returned, halo_sources, send, grad_nodes),
        [((width, width), BF16), ((count, width), BF16)],
        [((count, width), F32)],
    )
    vmem = pl.BlockSpec(memory_space=pltpu.VMEM)
    gradients = pl.pallas_call(
        reduce_phase,
        out_shape=jax.ShapeDtypeStruct((14, width, width), BF16),
        in_specs=[vmem] * 3,
        out_specs=vmem,
        scratch_shapes=reducer_scratch(14),
        compiler_params=pltpu.CompilerParams(collective_id=0, has_side_effects=True),
    )(grads1, grads0, last0)
    gradients = gradients.reshape(2, 7 * width, width)
    return nodes2[None], result[None], gradients


def solution(mesh):
    in_specs = (
        P("dp", "graph", None),
        P("graph", None),
        P("graph", None),
        P("graph", None, None),
        P("graph", None),
        P("graph", None),
        P("graph", None),
        P("graph", None),
        P("graph", None),
        P("graph", None),
        P(),
        P(),
        P(),
        P(),
        P(),
        P(),
        P("dp", "graph", None),
    )
    out_specs = (P("dp", "graph", None), P("dp", "graph", None), P())
    return jax.shard_map(
        on_device, mesh=mesh, in_specs=in_specs, out_specs=out_specs, check_vma=False
    )
```

```python
import functools
import math

import jax
import jax.numpy as jnp
from jax import lax
from jax.experimental import pallas as pl
from jax.experimental.pallas import tpu as pltpu
from jax.sharding import PartitionSpec as P

EPSILON = 1e-05
F32, BF16 = jnp.float32, jnp.bfloat16
LANES = 128
TILE = 256
WE, WS, WR, E2, PV, PA, N2 = range(7)


def mm(left, right):
    return jnp.dot(left, right, preferred_element_type=F32)


def mm_tn(left, right):
    return lax.dot_general(left, right, (((0,), (0,)), ((), ())), preferred_element_type=F32)


def mm_nt(left, right):
    return lax.dot_general(left, right, (((1,), (1,)), ((), ())), preferred_element_type=F32)


def iota(shape, axis):
    return lax.broadcasted_iota(jnp.int32, shape, axis)


def hot(condition):
    return jnp.where(condition, 1.0, 0.0).astype(BF16)


def sigmoid(x):
    return 0.5 * jnp.tanh(0.5 * x) + 0.5


def normalize(y):
    center = jnp.mean(y, axis=-1, keepdims=True)
    shifted = y - center
    inverse = lax.rsqrt(jnp.mean(shifted * shifted, axis=-1, keepdims=True) + EPSILON)
    return shifted * inverse, inverse


def normalize_back(normed, inverse, upstream):
    first = jnp.mean(upstream, axis=-1, keepdims=True)
    second = jnp.mean(upstream * normed, axis=-1, keepdims=True)
    return inverse * (upstream - first - normed * second)


def rows(start, size):
    return pl.ds(pl.multiple_of(start * size, size), size)


def block(which, width):
    return pl.ds(which * width, width)


def column(row):
    return jnp.transpose(jnp.broadcast_to(row, (LANES, LANES)))


def row_hot(row, width):
    index = column(row)
    lane = iota((LANES, LANES), 1)
    return [hot(index == lane + k * LANES) for k in range(width // LANES)]


def pack(values, tiles):
    count, width = values.shape
    parts = width // LANES
    at, of = iota((count * parts, count), 0), iota((count * parts, count), 1)
    total = None
    for c in range(parts):
        piece = mm(hot(at == of * parts + c), values[:, c * LANES : (c + 1) * LANES])
        total = piece if total is None else total + piece
    tiles[...] = total.astype(BF16)


def unpack(tiles, width):
    parts = width // LANES
    total = tiles.shape[0]
    of, at = iota((total // parts, total), 0), iota((total // parts, total), 1)
    whole = tiles[...]
    return jnp.concatenate(
        [mm(hot(at == of * parts + c), whole).astype(BF16) for c in range(parts)], axis=1
    )


AXES = (1, 1, 0, 2, 2, 0, 1, 0, 0, 2, 1, 1, 2, 0)


class Comm:
    def __init__(self, refs):
        (
            self.grads, self.result, self.half_in, self.quarter_in, self.tile_in, self.sent, self.got,
            self.ex_sent, self.ex_got,
        ) = refs
        self.graph, self.dp = lax.axis_index("graph"), lax.axis_index("dp")
        self.core = lax.rem(self.graph, 2)
        self.place = [lax.rem(self.graph // 2, 4), self.graph // 8, self.dp]

    def device(self, core, place):
        return (place[1] * 8 + place[0] * 2 + core, place[2])

    def partner(self):
        return self.device(1 - self.core, self.place)

    def peer(self, k):
        where = lax.rem(self.graph + k, 32)
        return where, (where, self.dp)

    def along(self, axis, k):
        place = list(self.place)
        place[axis] = lax.rem(place[axis] + k, 4)
        return place[axis], self.device(self.core, place)

    def over(self, axis, k):
        first, second = [a for a in range(3) if a != axis]
        where = lax.rem(self.place[first] * 4 + self.place[second] + k, 16)
        place = list(self.place)
        place[first], place[second] = where // 4, lax.rem(where, 4)
        return where, self.device(self.core, place)

    def greet(self):
        barrier = pltpu.get_barrier_semaphore()

        def signal(device):
            pl.semaphore_signal(barrier, inc=1, device_id=device, device_id_type=pl.DeviceIdType.MESH)

        def near(k, carry):
            signal(self.peer(k)[1])
            return carry

        def far(k, carry):
            signal(self.over(0, k)[1])
            signal(self.over(1, k)[1])
            return carry

        lax.fori_loop(1, 32, near, 0)
        lax.fori_loop(1, 16, far, 0)

    def greeted(self):
        pl.semaphore_wait(pltpu.get_barrier_semaphore(), 61)

    def copy(self, source, target, sent, got, device):
        pltpu.make_async_remote_copy(
            src_ref=source,
            dst_ref=target,
            send_sem=sent,
            recv_sem=got,
            device_id=device,
            device_id_type=pl.DeviceIdType.MESH,
        ).start()

    def send(self, b, stage, source, target, device):
        self.copy(source, target, self.sent.at[b, stage], self.got.at[b, stage], device)

    def wait_size(self, size, semaphore):
        pltpu.make_async_copy(size, size, semaphore).wait()

    def wait(self, semaphores, b, stage):
        sizes = (
            self.half_in.at[b], self.quarter_in.at[b], self.tile_in.at[b],
            self.tile_in.at[b], self.quarter_in.at[b], self.half_in.at[b],
        )
        self.wait_size(sizes[stage], semaphores.at[b, stage])

    def spot(self, where):
        at = pl.multiple_of((where // 4) * 16, 16)
        lane = pl.multiple_of(lax.rem(where, 4) * LANES, LANES)
        return at, lane

    def half_rows(self, core):
        return pl.ds(pl.multiple_of(core * 256, 256), 256)

    def quarter_rows(self, at):
        return pl.ds(pl.multiple_of(self.core * 256 + at * 64, 64), 64)

    def own_spot(self, b, k):
        where, device = self.over(AXES[b], k)
        at, lane = self.spot(where)
        base = self.core * 256 + self.place[AXES[b]] * 64
        return (pl.ds(pl.multiple_of(base + at, 16), 16), pl.ds(lane, LANES)), device

    def begin(self, b):
        other = self.half_rows(1 - self.core)
        self.send(b, 0, self.grads.at[b, other], self.half_in.at[b], self.partner())

    def step1(self, b):
        self.wait(self.got, b, 0)
        mine = self.half_rows(self.core)
        self.grads[b, mine, :] = (self.grads[b, mine, :].astype(F32) + self.half_in[b].astype(F32)).astype(BF16)
        for k in range(1, 4):
            at, device = self.along(AXES[b], k)
            self.send(b, 1, self.grads.at[b, self.quarter_rows(at)], self.quarter_in.at[b, k - 1], device)

    def step2(self, b):
        self.wait(self.got, b, 1)
        mine = self.quarter_rows(self.place[AXES[b]])
        total = self.grads[b, mine, :].astype(F32)
        for k in range(3):
            total = total + self.quarter_in[b, k].astype(F32)
        self.grads[b, mine, :] = total.astype(BF16)

        def one(k, carry):
            spot, device = self.own_spot(b, k)
            self.send(b, 2, self.grads.at[b, spot[0], spot[1]], self.tile_in.at[b, k - 1], device)
            return carry

        lax.fori_loop(1, 16, one, 0)

    def step3(self, b):
        self.wait(self.got, b, 2)
        spot, _ = self.own_spot(b, 0)
        total = self.grads[b, spot[0], spot[1]].astype(F32)
        total = total + jnp.sum(self.tile_in[b].astype(F32), axis=0)
        mine = self.result.at[b, spot[0], spot[1]]
        mine[...] = total.astype(BF16)

        def one(k, carry):
            self.send(b, 3, mine, mine, self.over(AXES[b], k)[1])
            return carry

        lax.fori_loop(1, 16, one, 0)

    def step4(self, b):
        self.wait(self.got, b, 3)
        mine = self.result.at[b, self.quarter_rows(self.place[AXES[b]])]
        for k in range(1, 4):
            self.send(b, 4, mine, mine, self.along(AXES[b], k)[1])

    def step5(self, b):
        self.wait(self.got, b, 4)
        mine = self.result.at[b, self.half_rows(self.core)]
        self.send(b, 5, mine, mine, self.partner())

    def step6(self, b):
        self.wait(self.got, b, 5)

    def leave(self, b):
        for stage in range(6):
            self.wait(self.sent, b, stage)

    def run(self, step, blocks):
        for b in blocks:
            (self.begin, self.step1, self.step2, self.step3, self.step4, self.step5, self.step6)[step](b)

    def exchange(self, e, out, into):
        mine = pl.ds(pl.multiple_of(self.graph * 16, 16), 16)
        into[mine, :] = out[mine, :]

        def one(k, carry):
            where, device = self.peer(k)
            theirs = pl.ds(pl.multiple_of(where * 16, 16), 16)
            self.copy(out.at[theirs], into.at[mine], self.ex_sent.at[e], self.ex_got.at[e], device)
            return carry

        lax.fori_loop(1, 32, one, 0)

    def exchanged(self, e, into):
        self.wait_size(into.at[pl.ds(0, 31 * 16)], self.ex_got.at[e])
        self.wait_size(into.at[pl.ds(0, 31 * 16)], self.ex_sent.at[e])


def messages_phase(comm, proj, geometry, geometry_weight, counts, sources, arrived):
    peers = counts.shape[1]
    capacity = 64
    grid_rows, width = proj.shape
    high = geometry_weight[...].astype(BF16)
    low = (geometry_weight[...] - high.astype(F32)).astype(BF16)
    count16 = jnp.broadcast_to(counts[...].astype(F32), (16, peers)).astype(BF16)
    home = comm.graph // 2
    target = arrived.at[pl.ds(pl.multiple_of(comm.graph * capacity, capacity), capacity)]

    def compute(chip):
        start = pl.multiple_of(chip * LANES, LANES)
        at = pl.ds(start, LANES)
        slot = start + iota((1, LANES), 1)
        owner = (start + iota((peers, LANES), 1)) // capacity
        limit = mm(count16, hot(owner == iota((peers, LANES), 0)))[:1]
        live = (slot % capacity).astype(F32) < limit
        index = jnp.where(live, sources[:, at], -1)
        shape = jnp.where(live, geometry[:, at].astype(F32), 0.0).astype(BF16)
        table = jnp.concatenate(row_hot(index, grid_rows), axis=1)
        pre = mm(table, proj[...]) + mm_tn(shape, high) + mm_tn(shape, low)
        where = (chip // 4, pl.ds(pl.multiple_of(lax.rem(chip, 4) * LANES, LANES), LANES))
        comm.grads[where[0], where[1], :] = (pre * sigmoid(pre)).astype(BF16)

    def part(chip, core):
        base = lax.rem(chip, 4) * LANES + core * capacity
        return comm.grads.at[chip // 4, pl.ds(pl.multiple_of(base, capacity), capacity)]

    def send(chip, core):
        comm.copy(
            part(chip, core), target, comm.ex_sent.at[4], comm.ex_got.at[4], (chip * 2 + core, comm.dp)
        )

    def step(k, carry):
        chip = lax.rem(home + k, 16)
        compute(chip)
        send(chip, 0)
        send(chip, 1)
        return carry

    lax.fori_loop(1, 16, step, 0)
    compute(home)
    send(home, 1 - comm.core)
    target[...] = part(home, comm.core)[...]


def tables_phase(senders, receivers, gather, scatter, extended):
    edges = senders.shape[1]
    nodes = gather.shape[1] - extended

    def step(i, carry):
        at = rows(i, LANES)
        send, recv = senders[:, at], receivers[:, at]
        gather[at, :extended] = jnp.concatenate(row_hot(send, extended), axis=1)
        gather[at, extended:] = jnp.concatenate(row_hot(recv, nodes), axis=1)
        scatter[:extended, at] = hot(iota((extended, LANES), 0) == send)
        scatter[extended:, at] = hot(iota((nodes, LANES), 0) == recv)
        return carry

    lax.fori_loop(0, edges // LANES, step, 0)


def halo_send(comm, e, nodes, picked, out, into):
    pack(mm(picked[...], nodes[...]).astype(BF16), out)
    comm.exchange(e, out, into)


def start_phase(arrived, targets, embed, message_weight, update, output, nodes, total):
    slots = targets.shape[1]
    count, width = embed.shape
    total[...] = jnp.zeros_like(total)

    def step(i, carry):
        at = rows(i, 2 * TILE)
        total[...] += mm(hot(iota((count, 2 * TILE), 0) == targets[:, at]), arrived[at, :])
        return carry

    lax.fori_loop(0, slots // (2 * TILE), step, 0)
    aggregate = mm(total[...].astype(BF16), message_weight[...]).astype(BF16)
    pre = mm(embed[...], update[0]) + mm(aggregate, update[1])
    normed, _ = normalize(mm((pre * sigmoid(pre)).astype(BF16), output[...]))
    nodes[...] = (embed[...].astype(F32) + normed).astype(BF16)


def forward_phase(comm, e, w, nodes, incoming, edges, gather, scatter, saved, new_nodes, proj, total, before):
    count, width = nodes.shape
    extended = gather.shape[1] - count
    proj[:count] = mm(nodes[...], w(WS)).astype(BF16)
    proj[extended:] = mm(nodes[...], w(WR)).astype(BF16)

    def early(i, carry):
        at = rows(i, TILE)
        before[at, :] = (
            mm(edges[at, :], w(WE))
            + mm(gather[at, :count], proj[:count])
            + mm(gather[at, extended:], proj[extended:])
        )
        return carry

    lax.fori_loop(0, edges.shape[0] // TILE, early, 0)
    comm.exchanged(e, incoming)
    proj[count:extended] = mm(unpack(incoming, width), w(WS)).astype(BF16)
    total[...] = jnp.zeros_like(total)

    def step(i, carry):
        at = rows(i, TILE)
        pre = before[at, :] + mm(gather[at, count:extended], proj[count:extended])
        s = sigmoid(pre)
        act = pre * s
        hid = act.astype(BF16)
        saved["hid"][at, :] = hid
        saved["slope"][at, :] = (s + act * (1.0 - s)).astype(BF16)
        normed, inverse = normalize(mm(hid, w(E2)))
        saved["normed"][at, :] = normed.astype(BF16)
        saved["inverse"][0][at, saved["inverse"][1]] = jnp.broadcast_to(inverse, (TILE, LANES // 2))
        new = (edges[at, :].astype(F32) + normed).astype(BF16)
        if saved["edges"] is not None:
            saved["edges"][at, :] = new
        total[...] += mm(scatter[extended:, at], new)
        return carry

    lax.fori_loop(0, edges.shape[0] // TILE, step, 0)
    summed = total[...].astype(BF16)
    pre = mm(nodes[...], w(PV)) + mm(summed, w(PA))
    s = sigmoid(pre)
    act = pre * s
    hid = act.astype(BF16)
    normed, inverse = normalize(mm(hid, w(N2)))
    new_nodes[...] = (nodes[...].astype(F32) + normed).astype(BF16)
    saved["summed"][...] = summed
    saved["node_hid"][...] = hid
    saved["node_slope"][...] = s + act * (1.0 - s)
    saved["node_normed"][...] = normed
    saved["node_inverse"][...] = jnp.broadcast_to(inverse, (count, LANES))


def backward_nodes(put, w, nodes, saved, grad_nodes, proj, extended):
    upstream = grad_nodes[...]
    q = normalize_back(saved["node_normed"][...], saved["node_inverse"][:, :1], upstream)
    q = q.astype(BF16)
    d_node = (mm_nt(q, w(N2)) * saved["node_slope"][...]).astype(BF16)
    proj[extended:] = mm_nt(d_node, w(PA)).astype(BF16)
    put(N2, mm_tn(saved["node_hid"][...], q))
    put(PV, mm_tn(nodes[...], d_node))
    put(PA, mm_tn(saved["summed"][...], d_node))
    grad_nodes[...] = upstream + mm_nt(d_node, w(PV))


def backward_edges(w, edges, gather, scatter, saved, grad_edges, first, last, proj, total, acc, extended, low, high):
    width = edges.shape[1]

    def step(i, carry):
        at = rows(i, TILE)
        up = mm(gather[at, extended:], proj[extended:])
        if not first:
            up = up + grad_edges[at, :]
        inverse = saved["inverse"][0][at, saved["inverse"][1]][:, :1]
        q = normalize_back(saved["normed"][at, :].astype(F32), inverse, up)
        q = q.astype(BF16)
        acc[width:] += mm_tn(saved["hid"][at, :], q)
        d = (mm_nt(q, w(E2)) * saved["slope"][at, :].astype(F32)).astype(BF16)
        acc[:width] += mm_tn(edges[at, :], d)
        total[...] += mm(scatter[:, at], d)
        if not last:
            grad_edges[at, :] = up + mm_nt(d, w(WE))
        return carry

    lax.fori_loop(low, high, step, 0)


SAVED = ("hid", "slope", "normed", "edges", "summed", "node_hid", "node_slope", "node_normed", "node_inverse")


def saved_shapes(edges, nodes, width, with_edges):
    shapes = {
        "hid": ((edges, width), BF16),
        "slope": ((edges, width), BF16),
        "normed": ((edges, width), BF16),
        "edges": ((edges, width), BF16),
        "summed": ((nodes, width), BF16),
        "node_hid": ((nodes, width), BF16),
        "node_slope": ((nodes, width), F32),
        "node_normed": ((nodes, width), F32),
        "node_inverse": ((nodes, LANES), F32),
    }
    return [shapes[name] for name in SAVED if with_edges or name != "edges"]


def saved_refs(refs, with_edges):
    names = [name for name in SAVED if with_edges or name != "edges"]
    found = dict(zip(names, refs))
    found.setdefault("edges", None)
    return found


def whole_kernel(
    scale,
    embed, geometry, counts, sources, targets, halo, senders, receivers, geometry_weight, cotangent,
    grid_any, grid_weight_any, message_weight_any, update_any, output_any, edges_any, weights_any,
    nodes2, mesh_gradient, result, *scratch,
):
    scratch = list(scratch)
    take = lambda n: [scratch.pop(0) for _ in range(n)]
    grads, half_in, quarter_in, tile_in, sent, got, ex_sent, ex_got, load = take(9)
    comm = Comm((grads, result, half_in, quarter_in, tile_in, sent, got, ex_sent, ex_got))
    arrived, edges, weights, gather, scatter, picked, nodes0, nodes1 = take(8)
    outs, ins = take(4), take(4)
    grad_edges, grad_nodes, proj, total, summing, acc = take(6)
    saved0 = saved_refs(take(len(SAVED)), True)
    saved1 = saved_refs(take(len(SAVED) - 1), False)
    (inverses,) = take(1)
    saved0["inverse"] = (inverses, slice(0, LANES // 2))
    saved1["inverse"] = (inverses, slice(LANES // 2, LANES))
    count, width = embed.shape
    extended = count + halo.shape[1]
    tiles = edges.shape[0] // TILE
    loads = [
        pltpu.make_async_copy(source, target, load.at[i])
        for i, (source, target) in enumerate(
            (
                (grid_any, grads.at[4]),
                (grid_weight_any, grads.at[5]),
                (message_weight_any, grads.at[6]),
                (output_any, grads.at[7]),
                (update_any, grads.at[pl.ds(8, 2)]),
                (edges_any, edges),
                (weights_any, weights),
            )
        )
    ]
    for copy in loads:
        copy.start()
    comm.greet()
    loads[0].wait()
    loads[1].wait()
    slots_proj = proj.at[pl.ds(0, grid_any.shape[0])]
    slots_proj[...] = mm(grads[4], grads[5]).astype(BF16)
    comm.greeted()
    messages_phase(comm, slots_proj, geometry, geometry_weight, counts, sources, arrived)
    tables_phase(senders, receivers, gather, scatter, extended)
    picked[...] = jnp.concatenate(row_hot(halo[...], count), axis=1)
    for copy in loads[2:]:
        copy.wait()
    comm.wait_size(arrived.at[pl.ds(0, 31 * 64)], ex_got.at[4])
    comm.wait_size(arrived.at[pl.ds(0, 31 * 64)], ex_sent.at[4])
    start_phase(arrived, targets, embed, grads.at[6], grads.at[pl.ds(8, 2)], grads.at[7], nodes0, summing)
    halo_send(comm, 0, nodes0, picked, outs[0], ins[0])

    def w0(which):
        return weights[block(which, width), :]

    def w1(which):
        return weights[block(7 + which, width), :]

    forward_phase(comm, 0, w0, nodes0, ins[0], edges, gather, scatter, saved0, nodes1, proj, summing, grad_edges)
    halo_send(comm, 1, nodes1, picked, outs[1], ins[1])
    edges1 = saved0["edges"]
    forward_phase(comm, 1, w1, nodes1, ins[1], edges1, gather, scatter, saved1, nodes2, proj, summing, grad_edges)
    grad_nodes[...] = cotangent[...].astype(F32)

    def putter(layer):
        def put(which, value):
            grads[layer * 7 + which] = (value * scale).astype(BF16)

        return put

    def blocks(layer, *which):
        return [layer * 7 + i for i in which]

    def clear():
        total[...] = jnp.zeros_like(total)
        acc[...] = jnp.zeros_like(acc)

    def edge_sums(put, w, nodes, e):
        pack(total[count:extended].astype(BF16), outs[e])
        comm.exchange(e, outs[e], ins[e])
        put(WE, acc[:width])
        put(E2, acc[width:])
        recv = total[extended:].astype(BF16)
        put(WR, mm_tn(nodes[...], recv))
        grad_nodes[...] += mm_nt(recv, w(WR))

    def finish(put, w, nodes, e):
        comm.exchanged(e, ins[e])
        back = hot(iota((count, halo.shape[1]), 0) == halo[...])
        send = (total[:count] + mm(back, unpack(ins[e], width))).astype(BF16)
        put(WS, mm_tn(nodes[...], send))
        grad_nodes[...] += mm_nt(send, w(WS))

    run = comm.run
    put1, put0 = putter(1), putter(0)
    backward_nodes(put1, w1, nodes1, saved1, grad_nodes, proj, extended)
    a1, b1, c1 = blocks(1, N2, PV, PA), blocks(1, WE, E2, WR), blocks(1, WS)
    a0, b0, c0 = blocks(0, N2, PV, PA), blocks(0, WE, E2, WR), blocks(0, WS)
    run(0, a1)
    clear()
    some = functools.partial(
        backward_edges, w1, edges1, gather, scatter, saved1, grad_edges, True, False, proj, total, acc, extended
    )
    some(0, tiles // 2)
    run(1, a1)
    some(tiles // 2, tiles)
    edge_sums(put1, w1, nodes1, 2)
    run(0, b1)
    run(2, a1)
    finish(put1, w1, nodes1, 2)
    run(0, c1)
    backward_nodes(put0, w0, nodes0, saved0, grad_nodes, proj, extended)
    run(0, a0)
    run(1, b1)
    run(3, a1)
    clear()
    some = functools.partial(
        backward_edges, w0, edges, gather, scatter, saved0, grad_edges, False, True, proj, total, acc, extended
    )
    some(0, tiles // 2)
    run(1, c1 + a0)
    run(2, b1)
    run(4, a1)
    some(tiles // 2, tiles)
    edge_sums(put0, w0, nodes0, 3)
    run(0, b0)
    run(2, c1 + a0)
    run(3, b1)
    run(5, a1)
    finish(put0, w0, nodes0, 3)
    run(0, c0)
    mesh_gradient[...] = grad_nodes[...].astype(BF16)
    run(1, b0)
    run(3, c1 + a0)
    run(4, b1)
    run(1, c0)
    run(2, b0)
    run(4, c1 + a0)
    run(5, b1)
    run(2, c0)
    run(3, b0)
    run(5, c1 + a0)
    run(3, c0)
    run(4, b0)
    run(4, c0)
    run(5, b0)
    run(5, c0)
    run(6, range(14))
    for b in range(14):
        comm.leave(b)


def on_device(
    grid_latent,
    mesh_embed,
    mesh_edges,
    edge_geometry,
    edge_counts,
    edge_sources,
    edge_targets,
    halo_sources,
    mesh_sources,
    mesh_targets,
    grid_weight,
    geometry_weight,
    message_weight,
    mesh_update,
    mesh_output,
    processor,
    cotangent,
):
    count, width = mesh_embed.shape
    edges = mesh_edges.shape[0]
    slots = edge_sources.shape[1]
    halo = halo_sources.shape[1]
    peers = lax.axis_size("graph")
    extended = count + halo
    table = extended + count
    tiles = (halo * width // LANES, LANES)
    scale = 1.0 / math.sqrt(lax.axis_size("dp") * peers * count)
    layers = processor.shape[0]
    vmem, anywhere = pl.BlockSpec(memory_space=pltpu.VMEM), pl.BlockSpec(memory_space=pl.ANY)
    dma = pltpu.SemaphoreType.DMA
    scratch = [
        ((7 * layers, width, width), BF16),
        ((7 * layers, width // 2, width), BF16),
        ((7 * layers, 3, width // 8, width), BF16),
        ((7 * layers, 15, 16, LANES), BF16),
        dma((7 * layers, 6)),
        dma((7 * layers, 6)),
        dma((5,)),
        dma((5,)),
        dma((7,)),
        ((slots, width), BF16),
        ((edges, width), BF16),
        ((7 * layers * width, width), BF16),
        ((edges, table), BF16),
        ((table, edges), BF16),
        ((halo, count), BF16),
        ((count, width), BF16),
        ((count, width), BF16),
        *[(tiles, BF16)] * 8,
        ((edges, width), F32),
        ((count, width), F32),
        ((table, width), BF16),
        ((table, width), F32),
        ((count, width), F32),
        ((2 * width, width), F32),
        *saved_shapes(edges, count, width, True),
        *saved_shapes(edges, count, width, False),
        ((edges, LANES), F32),
    ]
    nodes2, result, gradients = pl.pallas_call(
        functools.partial(whole_kernel, scale),
        out_shape=[
            jax.ShapeDtypeStruct((count, width), BF16),
            jax.ShapeDtypeStruct((count, width), BF16),
            jax.ShapeDtypeStruct((7 * layers, width, width), BF16),
        ],
        in_specs=[vmem] * 10 + [anywhere] * 7,
        out_specs=[vmem] * 3,
        scratch_shapes=[pltpu.VMEM(*item) if isinstance(item, tuple) else item for item in scratch],
        compiler_params=pltpu.CompilerParams(
            collective_id=0, has_side_effects=True, vmem_limit_bytes=67043328
        ),
    )(
        mesh_embed, edge_geometry[0], edge_counts, edge_sources, edge_targets, halo_sources, mesh_sources,
        mesh_targets, geometry_weight, cotangent[0],
        grid_latent[0], grid_weight, message_weight, mesh_update.reshape(2, width, width), mesh_output,
        mesh_edges, processor.reshape(-1, width),
    )
    return nodes2[None], result[None], gradients.reshape(processor.shape)


def solution(mesh):
    in_specs = (
        P("dp", "graph", None),
        P("graph", None),
        P("graph", None),
        P("graph", None, None),
        P("graph", None),
        P("graph", None),
        P("graph", None),
        P("graph", None),
        P("graph", None),
        P("graph", None),
        P(),
        P(),
        P(),
        P(),
        P(),
        P(),
        P("dp", "graph", None),
    )
    out_specs = (P("dp", "graph", None), P("dp", "graph", None), P())
    return jax.shard_map(
        on_device, mesh=mesh, in_specs=in_specs, out_specs=out_specs, check_vma=False
    )
```

```python
import functools
import math

import jax
import jax.numpy as jnp
from jax import lax
from jax.experimental import pallas as pl
from jax.experimental.pallas import tpu as pltpu
from jax.sharding import PartitionSpec as P

EPSILON = 1e-05
F32, BF16 = jnp.float32, jnp.bfloat16
LANES = 128
TILE = 512
WE, WS, WR, E2, PV, PA, N2 = range(7)


def mm(left, right):
    return jnp.dot(left, right, preferred_element_type=F32)


def mm_tn(left, right):
    return lax.dot_general(left, right, (((0,), (0,)), ((), ())), preferred_element_type=F32)


def mm_nt(left, right):
    return lax.dot_general(left, right, (((1,), (1,)), ((), ())), preferred_element_type=F32)


def iota(shape, axis):
    return lax.broadcasted_iota(jnp.int32, shape, axis)


def hot(condition):
    return jnp.where(condition, 1.0, 0.0).astype(BF16)


def sigmoid(x):
    return 0.5 * jnp.tanh(0.5 * x) + 0.5


def normalize(y):
    center = jnp.mean(y, axis=-1, keepdims=True)
    shifted = y - center
    inverse = lax.rsqrt(jnp.mean(shifted * shifted, axis=-1, keepdims=True) + EPSILON)
    return shifted * inverse, inverse


def normalize_back(normed, inverse, upstream):
    first = jnp.mean(upstream, axis=-1, keepdims=True)
    second = jnp.mean(upstream * normed, axis=-1, keepdims=True)
    return inverse * (upstream - first - normed * second)


def rows(start, size):
    return pl.ds(pl.multiple_of(start * size, size), size)


def block(which, width):
    return pl.ds(which * width, width)


def column(row):
    return jnp.transpose(jnp.broadcast_to(row, (LANES, LANES)))


def row_hot(row, width):
    index = column(row)
    lane = iota((LANES, LANES), 1)
    return [hot(index == lane + k * LANES) for k in range(width // LANES)]


def pack(values, tiles):
    count, width = values.shape
    parts = width // LANES
    at, of = iota((count * parts, count), 0), iota((count * parts, count), 1)
    total = None
    for c in range(parts):
        piece = mm(hot(at == of * parts + c), values[:, c * LANES : (c + 1) * LANES])
        total = piece if total is None else total + piece
    tiles[...] = total.astype(BF16)


def unpack(tiles, width):
    parts = width // LANES
    total = tiles.shape[0]
    of, at = iota((total // parts, total), 0), iota((total // parts, total), 1)
    whole = tiles[...]
    return jnp.concatenate(
        [mm(hot(at == of * parts + c), whole).astype(BF16) for c in range(parts)], axis=1
    )


STAGES = 8
AXES = (0, 1, 2, 0, 2, 0, 1, 0, 1, 2, 1, 1, 2, 0)


FIRST = ((2, 0), (0, 2), (2, 1), (1, 2), (2, 2), (3, 2), (2, 3))
THEN = ((1, 1), (3, 1), (1, 3), (3, 3), (1, 0), (3, 0), (0, 1), (0, 3))


class Comm:
    def __init__(self, refs):
        (
            self.grads, self.result, self.half_in, self.quarter_in, self.tile_in, self.sent, self.got,
            self.ex_sent, self.ex_got,
        ) = refs
        self.graph, self.dp = lax.axis_index("graph"), lax.axis_index("dp")
        self.core = lax.rem(self.graph, 2)
        self.place = [lax.rem(self.graph // 2, 4), self.graph // 8, self.dp]
        self.spots = [[self.find_spot(axis, k) for k in range(16)] for axis in range(3)]

    def device(self, core, place):
        return (place[1] * 8 + place[0] * 2 + core, place[2])

    def partner(self):
        return self.device(1 - self.core, self.place)

    def peer(self, k):
        where = lax.rem(self.graph + k, 32)
        return where, (where, self.dp)

    def chip(self, dx, dy):
        return lax.rem(self.place[1] + dy, 4) * 4 + lax.rem(self.place[0] + dx, 4)

    def along(self, axis, k):
        place = list(self.place)
        place[axis] = lax.rem(place[axis] + k, 4)
        return place[axis], self.device(self.core, place)

    def over(self, axis, k):
        first, second = [a for a in range(3) if a != axis]
        where = lax.rem(self.place[first] * 4 + self.place[second] + k, 16)
        place = list(self.place)
        place[first], place[second] = where // 4, lax.rem(where, 4)
        return where, self.device(self.core, place)

    def greet(self):
        barrier = pltpu.get_barrier_semaphore()

        def signal(device):
            pl.semaphore_signal(barrier, inc=1, device_id=device, device_id_type=pl.DeviceIdType.MESH)

        def near(k, carry):
            signal(self.peer(k)[1])
            return carry

        def far(k, carry):
            signal(self.over(0, k)[1])
            signal(self.over(1, k)[1])
            return carry

        lax.fori_loop(1, 32, near, 0)
        lax.fori_loop(1, 16, far, 0)

    def greeted(self):
        pl.semaphore_wait(pltpu.get_barrier_semaphore(), 61)

    def copy(self, source, target, sent, got, device):
        pltpu.make_async_remote_copy(
            src_ref=source,
            dst_ref=target,
            send_sem=sent,
            recv_sem=got,
            device_id=device,
            device_id_type=pl.DeviceIdType.MESH,
        ).start()

    def send(self, b, stage, source, target, device):
        self.copy(source, target, self.sent.at[b, stage], self.got.at[b, stage], device)

    def wait_size(self, size, semaphore):
        pltpu.make_async_copy(size, size, semaphore).wait()

    def wait(self, semaphores, b, stage):
        whole, half, full, tiles = (
            self.half_in.at[b], self.quarter_in.at[b, 2], self.quarter_in.at[b, pl.ds(0, 2)], self.tile_in.at[b]
        )
        sizes = (whole, half, full, tiles, tiles, full, half, whole)
        self.wait_size(sizes[stage], semaphores.at[b, stage])

    def spot(self, where):
        at = pl.multiple_of((where // 4) * 16, 16)
        lane = pl.multiple_of(lax.rem(where, 4) * LANES, LANES)
        return at, lane

    def half_rows(self, core):
        return pl.ds(pl.multiple_of(core * 256, 256), 256)

    def quarter_rows(self, at):
        return pl.ds(pl.multiple_of(self.core * 256 + at * 64, 64), 64)

    def find_spot(self, axis, k):
        where, device = self.over(axis, k)
        at, lane = self.spot(where)
        return pl.multiple_of(self.core * 256 + self.place[axis] * 64 + at, 16), lane, device

    def own_spot(self, b, k):
        at, lane, device = self.spots[AXES[b]][k]
        return (pl.ds(at, 16), pl.ds(lane, LANES)), device

    def begin(self, b):
        other = self.half_rows(1 - self.core)
        self.send(b, 0, self.grads.at[b, other], self.half_in.at[b], self.partner())

    def part(self, b, k, half):
        base = self.core * 256 + self.along(AXES[b], k)[0] * 64
        size = 64 if half is None else 32
        return pl.ds(pl.multiple_of(base + (32 if half == 1 else 0), size), size)

    def step1(self, b):
        self.wait(self.got, b, 0)
        mine = self.half_rows(self.core)
        self.grads[b, mine, :] = (self.grads[b, mine, :].astype(F32) + self.half_in[b].astype(F32)).astype(BF16)
        for half, k in ((0, 1), (1, 3)):
            target = self.quarter_in.at[b, 2, pl.ds(half * 32, 32)]
            self.send(b, 1, self.grads.at[b, self.part(b, 2, half)], target, self.along(AXES[b], k)[1])

    def step2(self, b):
        self.wait(self.got, b, 1)
        for half, k in ((0, 1), (1, 3)):
            mine = self.part(b, k, half)
            more = self.quarter_in[b, 2, pl.ds(half * 32, 32), :].astype(F32)
            self.grads[b, mine, :] = (self.grads[b, mine, :].astype(F32) + more).astype(BF16)
            self.send(
                b, 2, self.grads.at[b, self.part(b, k, None)], self.quarter_in.at[b, half], self.along(AXES[b], k)[1]
            )

    def step3(self, b):
        self.wait(self.got, b, 2)
        mine = self.part(b, 0, None)
        total = self.grads[b, mine, :].astype(F32)
        for k in range(2):
            total = total + self.quarter_in[b, k].astype(F32)
        self.grads[b, mine, :] = total.astype(BF16)

        for k in range(1, 16):
            spot, device = self.own_spot(b, k)
            self.send(b, 3, self.grads.at[b, spot[0], spot[1]], self.tile_in.at[b, k - 1], device)

    def step4(self, b):
        self.wait(self.got, b, 3)
        spot, _ = self.own_spot(b, 0)
        total = self.grads[b, spot[0], spot[1]].astype(F32)
        total = total + jnp.sum(self.tile_in[b].astype(F32), axis=0)
        mine = self.result.at[b, spot[0], spot[1]]
        mine[...] = total.astype(BF16)

        for k in range(1, 16):
            self.send(b, 4, mine, mine, self.own_spot(b, k)[1])

    def step5(self, b):
        self.wait(self.got, b, 4)
        mine = self.result.at[b, self.part(b, 0, None)]
        for k in (1, 3):
            self.send(b, 5, mine, mine, self.along(AXES[b], k)[1])

    def step6(self, b):
        self.wait(self.got, b, 5)
        for half, k in ((0, 1), (1, 3)):
            other = self.result.at[b, self.part(b, 4 - k, half)]
            self.send(b, 6, other, other, self.along(AXES[b], k)[1])

    def step7(self, b):
        self.wait(self.got, b, 6)
        mine = self.result.at[b, self.half_rows(self.core)]
        self.send(b, 7, mine, mine, self.partner())

    def step8(self, b):
        self.wait(self.got, b, 7)

    def leave(self, b):
        for stage in range(STAGES):
            self.wait(self.sent, b, stage)

    def run(self, step, blocks):
        steps = (
            self.begin, self.step1, self.step2, self.step3, self.step4, self.step5, self.step6, self.step7, self.step8
        )
        for b in blocks:
            steps[step](b)

    def exchange(self, e, out, into):
        mine = pl.ds(pl.multiple_of(self.graph * 16, 16), 16)
        into[mine, :] = out[mine, :]

        def one(k, carry):
            where, device = self.peer(k)
            theirs = pl.ds(pl.multiple_of(where * 16, 16), 16)
            self.copy(out.at[theirs], into.at[mine], self.ex_sent.at[e], self.ex_got.at[e], device)
            return carry

        lax.fori_loop(1, 32, one, 0)

    def exchanged(self, e, into):
        self.wait_size(into.at[pl.ds(0, 31 * 16)], self.ex_got.at[e])
        self.wait_size(into.at[pl.ds(0, 31 * 16)], self.ex_sent.at[e])


def messages_phase(comm, proj, geometry, geometry_weight, counts, sources, arrived):
    peers = counts.shape[1]
    capacity = 64
    grid_rows, width = proj.shape
    high = geometry_weight[...].astype(BF16)
    low = (geometry_weight[...] - high.astype(F32)).astype(BF16)
    count16 = jnp.broadcast_to(counts[...].astype(F32), (16, peers)).astype(BF16)
    home = comm.graph // 2
    target = arrived.at[pl.ds(pl.multiple_of(comm.graph * capacity, capacity), capacity)]

    def compute(chip):
        start = pl.multiple_of(chip * LANES, LANES)
        at = pl.ds(start, LANES)
        slot = start + iota((1, LANES), 1)
        owner = (start + iota((peers, LANES), 1)) // capacity
        limit = mm(count16, hot(owner == iota((peers, LANES), 0)))[:1]
        live = (slot % capacity).astype(F32) < limit
        index = jnp.where(live, sources[:, at], -1)
        shape = jnp.where(live, geometry[:, at].astype(F32), 0.0).astype(BF16)
        table = jnp.concatenate(row_hot(index, grid_rows), axis=1)
        pre = mm(table, proj[...]) + mm_tn(shape, high) + mm_tn(shape, low)
        where = (chip // 4, pl.ds(pl.multiple_of(lax.rem(chip, 4) * LANES, LANES), LANES))
        comm.grads[where[0], where[1], :] = (pre * sigmoid(pre)).astype(BF16)

    def part(chip, core):
        base = lax.rem(chip, 4) * LANES + core * capacity
        return comm.grads.at[chip // 4, pl.ds(pl.multiple_of(base, capacity), capacity)]

    def send(chip, core):
        comm.copy(
            part(chip, core), target, comm.ex_sent.at[4], comm.ex_got.at[4], (chip * 2 + core, comm.dp)
        )

    for dx, dy in FIRST + THEN:
        chip = comm.chip(dx, dy)
        compute(chip)
        send(chip, 1 - comm.core)
        send(chip, comm.core)
    compute(home)
    send(home, 1 - comm.core)
    target[...] = part(home, comm.core)[...]


def tables_phase(senders, receivers, gather, scatter, extended):
    edges = senders.shape[1]
    nodes = gather.shape[1] - extended

    def step(i, carry):
        at = rows(i, LANES)
        send, recv = senders[:, at], receivers[:, at]
        gather[at, :extended] = jnp.concatenate(row_hot(send, extended), axis=1)
        gather[at, extended:] = jnp.concatenate(row_hot(recv, nodes), axis=1)
        scatter[:extended, at] = hot(iota((extended, LANES), 0) == send)
        scatter[extended:, at] = hot(iota((nodes, LANES), 0) == recv)
        return carry

    lax.fori_loop(0, edges // LANES, step, 0)


def halo_send(comm, e, nodes, picked, out, into):
    pack(mm(picked[...], nodes[...]).astype(BF16), out)
    comm.exchange(e, out, into)


def start_phase(arrived, targets, embed, message_weight, update, output, nodes, total):
    slots = targets.shape[1]
    count, width = embed.shape
    total[...] = jnp.zeros_like(total)

    def step(i, carry):
        at = rows(i, TILE)
        total[...] += mm(hot(iota((count, TILE), 0) == targets[:, at]), arrived[at, :])
        return carry

    lax.fori_loop(0, slots // TILE, step, 0)
    aggregate = mm(total[...].astype(BF16), message_weight[...]).astype(BF16)
    pre = mm(embed[...], update[0]) + mm(aggregate, update[1])
    normed, _ = normalize(mm((pre * sigmoid(pre)).astype(BF16), output[...]))
    nodes[...] = (embed[...].astype(F32) + normed).astype(BF16)


def forward_phase(comm, e, w, nodes, incoming, edges, gather, scatter, saved, new_nodes, proj, total, before):
    count, width = nodes.shape
    extended = gather.shape[1] - count
    proj[:count] = mm(nodes[...], w(WS)).astype(BF16)
    proj[extended:] = mm(nodes[...], w(WR)).astype(BF16)

    def early(i, carry):
        at = rows(i, TILE)
        before[at, :] = (
            mm(edges[at, :], w(WE))
            + mm(gather[at, :count], proj[:count])
            + mm(gather[at, extended:], proj[extended:])
        )
        return carry

    lax.fori_loop(0, edges.shape[0] // TILE, early, 0)
    comm.exchanged(e, incoming)
    proj[count:extended] = mm(unpack(incoming, width), w(WS)).astype(BF16)
    total[...] = jnp.zeros_like(total)

    def step(i, carry):
        at = rows(i, TILE)
        pre = before[at, :] + mm(gather[at, count:extended], proj[count:extended])
        s = sigmoid(pre)
        act = pre * s
        hid = act.astype(BF16)
        saved["hid"][at, :] = hid
        saved["slope"][at, :] = (s + act * (1.0 - s)).astype(BF16)
        normed, inverse = normalize(mm(hid, w(E2)))
        saved["normed"][at, :] = normed.astype(BF16)
        saved["inverse"][0][at, saved["inverse"][1]] = jnp.broadcast_to(inverse, (TILE, LANES // 2))
        new = (edges[at, :].astype(F32) + normed).astype(BF16)
        if saved["edges"] is not None:
            saved["edges"][at, :] = new
        total[...] += mm(scatter[extended:, at], new)
        return carry

    lax.fori_loop(0, edges.shape[0] // TILE, step, 0)
    summed = total[...].astype(BF16)
    pre = mm(nodes[...], w(PV)) + mm(summed, w(PA))
    s = sigmoid(pre)
    act = pre * s
    hid = act.astype(BF16)
    normed, inverse = normalize(mm(hid, w(N2)))
    new_nodes[...] = (nodes[...].astype(F32) + normed).astype(BF16)
    saved["summed"][...] = summed
    saved["node_hid"][...] = hid
    saved["node_slope"][...] = s + act * (1.0 - s)
    saved["node_normed"][...] = normed
    saved["node_inverse"][...] = jnp.broadcast_to(inverse, (count, LANES))


def backward_nodes(put, w, nodes, saved, grad_nodes, proj, extended):
    upstream = grad_nodes[...]
    q = normalize_back(saved["node_normed"][...], saved["node_inverse"][:, :1], upstream)
    q = q.astype(BF16)
    d_node = (mm_nt(q, w(N2)) * saved["node_slope"][...]).astype(BF16)
    proj[extended:] = mm_nt(d_node, w(PA)).astype(BF16)
    put(N2, mm_tn(saved["node_hid"][...], q))
    put(PV, mm_tn(nodes[...], d_node))
    put(PA, mm_tn(saved["summed"][...], d_node))
    grad_nodes[...] = upstream + mm_nt(d_node, w(PV))


def backward_inner(gather, saved, grad_edges, first, last, proj, acc, extended, low, high):
    def step(i, carry):
        at = rows(i, TILE)
        up = mm(gather[at, extended:], proj[extended:])
        if not first:
            up = up + grad_edges[at, :]
        inverse = saved["inverse"][0][at, saved["inverse"][1]][:, :1]
        q = normalize_back(saved["normed"][at, :].astype(F32), inverse, up)
        q = q.astype(BF16)
        acc[...] += mm_tn(saved["hid"][at, :], q)
        saved["hid"][at, :] = q
        if not last:
            grad_edges[at, :] = up
        return carry

    lax.fori_loop(low, high, step, 0)


def backward_outer(w, edges, scatter, saved, grad_edges, last, total, acc, low, high):
    def step(i, carry):
        at = rows(i, TILE)
        d = (mm_nt(saved["hid"][at, :], w(E2)) * saved["slope"][at, :].astype(F32)).astype(BF16)
        acc[...] += mm_tn(edges[at, :], d)
        total[...] += mm(scatter[:, at], d)
        if not last:
            grad_edges[at, :] += mm_nt(d, w(WE))
        return carry

    lax.fori_loop(low, high, step, 0)


SAVED = ("hid", "slope", "normed", "edges", "summed", "node_hid", "node_slope", "node_normed", "node_inverse")


def saved_shapes(edges, nodes, width, with_edges):
    shapes = {
        "hid": ((edges, width), BF16),
        "slope": ((edges, width), BF16),
        "normed": ((edges, width), BF16),
        "edges": ((edges, width), BF16),
        "summed": ((nodes, width), BF16),
        "node_hid": ((nodes, width), BF16),
        "node_slope": ((nodes, width), F32),
        "node_normed": ((nodes, width), F32),
        "node_inverse": ((nodes, LANES), F32),
    }
    return [shapes[name] for name in SAVED if with_edges or name != "edges"]


def saved_refs(refs, with_edges):
    names = [name for name in SAVED if with_edges or name != "edges"]
    found = dict(zip(names, refs))
    found.setdefault("edges", None)
    return found


def whole_kernel(
    scale,
    embed, geometry, counts, sources, targets, halo, senders, receivers, geometry_weight, cotangent,
    grid_any, grid_weight_any, message_weight_any, update_any, output_any, edges_any, weights_any,
    nodes2, mesh_gradient, result, *scratch,
):
    scratch = list(scratch)
    take = lambda n: [scratch.pop(0) for _ in range(n)]
    grads, half_in, quarter_in, tile_in, sent, got, ex_sent, ex_got, load = take(9)
    comm = Comm((grads, result, half_in, quarter_in, tile_in, sent, got, ex_sent, ex_got))
    arrived, edges, weights, gather, scatter, picked, nodes0, nodes1 = take(8)
    outs, ins = take(4), take(4)
    grad_edges, grad_nodes, proj, total, summing, acc_inner, acc_outer = take(7)
    saved0 = saved_refs(take(len(SAVED)), True)
    saved1 = saved_refs(take(len(SAVED) - 1), False)
    (inverses,) = take(1)
    saved0["inverse"] = (inverses, slice(0, LANES // 2))
    saved1["inverse"] = (inverses, slice(LANES // 2, LANES))
    count, width = embed.shape
    extended = count + halo.shape[1]
    tiles = edges.shape[0] // TILE
    loads = [
        pltpu.make_async_copy(source, target, load.at[i])
        for i, (source, target) in enumerate(
            (
                (grid_any, grads.at[4]),
                (grid_weight_any, grads.at[5]),
                (message_weight_any, grads.at[6]),
                (output_any, grads.at[7]),
                (update_any, grads.at[pl.ds(8, 2)]),
                (edges_any, edges),
                (weights_any, weights),
            )
        )
    ]
    for copy in loads:
        copy.start()
    comm.greet()
    loads[0].wait()
    loads[1].wait()
    slots_proj = proj.at[pl.ds(0, grid_any.shape[0])]
    slots_proj[...] = mm(grads[4], grads[5]).astype(BF16)
    comm.greeted()
    messages_phase(comm, slots_proj, geometry, geometry_weight, counts, sources, arrived)
    tables_phase(senders, receivers, gather, scatter, extended)
    picked[...] = jnp.concatenate(row_hot(halo[...], count), axis=1)
    for copy in loads[2:]:
        copy.wait()
    comm.wait_size(arrived.at[pl.ds(0, 31 * 64)], ex_got.at[4])
    start_phase(arrived, targets, embed, grads.at[6], grads.at[pl.ds(8, 2)], grads.at[7], nodes0, summing)
    halo_send(comm, 0, nodes0, picked, outs[0], ins[0])

    def w0(which):
        return weights[block(which, width), :]

    def w1(which):
        return weights[block(7 + which, width), :]

    forward_phase(comm, 0, w0, nodes0, ins[0], edges, gather, scatter, saved0, nodes1, proj, summing, grad_edges)
    halo_send(comm, 1, nodes1, picked, outs[1], ins[1])
    edges1 = saved0["edges"]
    forward_phase(comm, 1, w1, nodes1, ins[1], edges1, gather, scatter, saved1, nodes2, proj, summing, grad_edges)
    grad_nodes[...] = cotangent[...].astype(F32)

    def putter(layer):
        def put(which, value):
            grads[layer * 7 + which] = (value * scale).astype(BF16)

        return put

    def blocks(layer, *which):
        return [layer * 7 + i for i in which]

    def clear():
        total[...] = jnp.zeros_like(total)
        acc_inner[...] = jnp.zeros_like(acc_inner)
        acc_outer[...] = jnp.zeros_like(acc_outer)

    def edge_sums(put, w, nodes, e, incoming):
        outer = total[count:extended].astype(BF16)
        pack(outer, outs[e])
        comm.exchange(e, outs[e], ins[e])
        put(WE, acc_outer[...])
        recv = total[extended:].astype(BF16)
        put(WR, mm_tn(nodes[...], recv))
        put(WS, mm_tn(nodes[...], total[:count].astype(BF16)) + mm_tn(unpack(incoming, width), outer))
        grad_nodes[...] += mm_nt(recv, w(WR))

    def finish(w, e):
        comm.exchanged(e, ins[e])
        back = hot(iota((count, halo.shape[1]), 0) == halo[...])
        send = (total[:count] + mm(back, unpack(ins[e], width))).astype(BF16)
        grad_nodes[...] += mm_nt(send, w(WS))

    run = comm.run
    put1, put0 = putter(1), putter(0)
    a1, e1, b1 = blocks(1, N2, PV, PA), blocks(1, E2), blocks(1, WE, WR, WS)
    a0, e0, b0 = blocks(0, N2, PV, PA), blocks(0, E2), blocks(0, WE, WR, WS)
    comm.wait_size(arrived.at[pl.ds(0, 31 * 64)], ex_sent.at[4])

    pieces = [(i * tiles // 3, (i + 1) * tiles // 3) for i in range(3)]

    def inner(piece, saved, first, last):
        backward_inner(gather, saved, grad_edges, first, last, proj, acc_inner, extended, *pieces[piece])

    def outer(piece, w, edges, saved, last):
        backward_outer(w, edges, scatter, saved, grad_edges, last, total, acc_outer, *pieces[piece])

    clear()
    backward_nodes(put1, w1, nodes1, saved1, grad_nodes, proj, extended)
    run(0, a1)
    inner(0, saved1, True, False)
    inner(1, saved1, True, False)
    inner(2, saved1, True, False)
    put1(E2, acc_inner[...])
    run(0, e1)
    run(1, a1)
    outer(0, w1, edges1, saved1, False)
    outer(1, w1, edges1, saved1, False)
    run(1, e1)
    outer(2, w1, edges1, saved1, False)
    run(2, a1)
    edge_sums(put1, w1, nodes1, 2, ins[1])
    run(0, b1)
    run(2, e1)
    finish(w1, 2)
    run(3, a1)
    clear()
    backward_nodes(put0, w0, nodes0, saved0, grad_nodes, proj, extended)
    run(0, a0)
    run(1, b1)
    run(3, e1)
    inner(0, saved0, False, True)
    inner(1, saved0, False, True)
    inner(2, saved0, False, True)
    put0(E2, acc_inner[...])
    run(0, e0)
    run(1, a0)
    run(4, a1)
    outer(0, w0, edges, saved0, True)
    run(2, b1)
    run(4, e1)
    outer(1, w0, edges, saved0, True)
    run(1, e0)
    outer(2, w0, edges, saved0, True)
    run(2, a0)
    edge_sums(put0, w0, nodes0, 3, ins[0])
    run(0, b0)
    run(5, a1)
    run(5, e1)
    run(3, b1)
    run(2, e0)
    run(1, b0)
    run(3, a0)
    finish(w0, 3)
    mesh_gradient[...] = grad_nodes[...].astype(BF16)
    run(2, b0)
    run(4, b1)
    run(3, e0)
    run(6, a1)
    run(6, e1)
    run(3, b0)
    run(4, a0)
    run(4, e0)
    run(7, a1)
    run(7, e1)
    run(5, b1)
    run(4, b0)
    run(5, a0)
    run(5, e0)
    run(6, b1)
    run(5, b0)
    run(6, a0)
    run(6, e0)
    run(7, b1)
    run(6, b0)
    run(7, a0)
    run(7, e0)
    run(7, b0)
    run(8, range(14))
    for b in range(14):
        comm.leave(b)


def on_device(
    grid_latent,
    mesh_embed,
    mesh_edges,
    edge_geometry,
    edge_counts,
    edge_sources,
    edge_targets,
    halo_sources,
    mesh_sources,
    mesh_targets,
    grid_weight,
    geometry_weight,
    message_weight,
    mesh_update,
    mesh_output,
    processor,
    cotangent,
):
    count, width = mesh_embed.shape
    edges = mesh_edges.shape[0]
    slots = edge_sources.shape[1]
    halo = halo_sources.shape[1]
    peers = lax.axis_size("graph")
    extended = count + halo
    table = extended + count
    tiles = (halo * width // LANES, LANES)
    scale = 1.0 / math.sqrt(lax.axis_size("dp") * peers * count)
    layers = processor.shape[0]
    vmem, anywhere = pl.BlockSpec(memory_space=pltpu.VMEM), pl.BlockSpec(memory_space=pl.ANY)
    dma = pltpu.SemaphoreType.DMA
    scratch = [
        ((7 * layers, width, width), BF16),
        ((7 * layers, width // 2, width), BF16),
        ((7 * layers, 3, width // 8, width), BF16),
        ((7 * layers, 15, 16, LANES), BF16),
        dma((7 * layers, STAGES)),
        dma((7 * layers, STAGES)),
        dma((5,)),
        dma((5,)),
        dma((7,)),
        ((slots, width), BF16),
        ((edges, width), BF16),
        ((7 * layers * width, width), BF16),
        ((edges, table), BF16),
        ((table, edges), BF16),
        ((halo, count), BF16),
        ((count, width), BF16),
        ((count, width), BF16),
        *[(tiles, BF16)] * 8,
        ((edges, width), F32),
        ((count, width), F32),
        ((table, width), BF16),
        ((table, width), F32),
        ((count, width), F32),
        ((width, width), F32),
        ((width, width), F32),
        *saved_shapes(edges, count, width, True),
        *saved_shapes(edges, count, width, False),
        ((edges, LANES), F32),
    ]
    nodes2, result, gradients = pl.pallas_call(
        functools.partial(whole_kernel, scale),
        out_shape=[
            pltpu.VMEM((count, width), BF16),
            pltpu.VMEM((count, width), BF16),
            pltpu.VMEM((7 * layers, width, width), BF16),
        ],
        in_specs=[vmem] * 10 + [anywhere] * 7,
        out_specs=[vmem] * 3,
        scratch_shapes=[pltpu.VMEM(*item) if isinstance(item, tuple) else item for item in scratch],
        compiler_params=pltpu.CompilerParams(
            collective_id=0, has_side_effects=True, vmem_limit_bytes=59100000
        ),
    )(
        mesh_embed, edge_geometry[0], edge_counts, edge_sources, edge_targets, halo_sources, mesh_sources,
        mesh_targets, geometry_weight, cotangent[0],
        grid_latent[0], grid_weight, message_weight, mesh_update.reshape(2, width, width), mesh_output,
        mesh_edges, processor.reshape(-1, width),
    )
    return nodes2[None], result[None], gradients.reshape(processor.shape)


def solution(mesh):
    in_specs = (
        P("dp", "graph", None),
        P("graph", None),
        P("graph", None),
        P("graph", None, None),
        P("graph", None),
        P("graph", None),
        P("graph", None),
        P("graph", None),
        P("graph", None),
        P("graph", None),
        P(),
        P(),
        P(),
        P(),
        P(),
        P(),
        P("dp", "graph", None),
    )
    out_specs = (P("dp", "graph", None), P("dp", "graph", None), P())
    return jax.shard_map(
        on_device, mesh=mesh, in_specs=in_specs, out_specs=out_specs, check_vma=False
    )
```

```python
import functools
import math

import jax
import jax.numpy as jnp
from jax import lax
from jax.experimental import pallas as pl
from jax.experimental.pallas import tpu as pltpu
from jax.sharding import PartitionSpec as P

EPSILON = 1e-05
F32, BF16 = jnp.float32, jnp.bfloat16
LANES = 128
TILE = 512
WE, WS, WR, E2, PV, PA, N2 = range(7)


def mm(left, right):
    return jnp.dot(left, right, preferred_element_type=F32)


def mm_tn(left, right):
    return lax.dot_general(left, right, (((0,), (0,)), ((), ())), preferred_element_type=F32)


def mm_nt(left, right):
    return lax.dot_general(left, right, (((1,), (1,)), ((), ())), preferred_element_type=F32)


def iota(shape, axis):
    return lax.broadcasted_iota(jnp.int32, shape, axis)


def hot(condition):
    return jnp.where(condition, 1.0, 0.0).astype(BF16)


def sigmoid(x):
    return 0.5 * jnp.tanh(0.5 * x) + 0.5


def normalize(y):
    center = jnp.mean(y, axis=-1, keepdims=True)
    shifted = y - center
    inverse = lax.rsqrt(jnp.mean(shifted * shifted, axis=-1, keepdims=True) + EPSILON)
    return shifted * inverse, inverse


def normalize_back(normed, inverse, upstream):
    first = jnp.mean(upstream, axis=-1, keepdims=True)
    second = jnp.mean(upstream * normed, axis=-1, keepdims=True)
    return inverse * (upstream - first - normed * second)


def rows(start, size):
    return pl.ds(pl.multiple_of(start * size, size), size)


def block(which, width):
    return pl.ds(which * width, width)


def column(row):
    return jnp.transpose(jnp.broadcast_to(row, (LANES, LANES)))


def row_hot(row, width):
    index = column(row)
    lane = iota((LANES, LANES), 1)
    return [hot(index == lane + k * LANES) for k in range(width // LANES)]


def pack(values, tiles):
    count, width = values.shape
    parts = width // LANES
    at, of = iota((count * parts, count), 0), iota((count * parts, count), 1)
    total = None
    for c in range(parts):
        piece = mm(hot(at == of * parts + c), values[:, c * LANES : (c + 1) * LANES])
        total = piece if total is None else total + piece
    tiles[...] = total.astype(BF16)


def unpack(tiles, width):
    parts = width // LANES
    total = tiles.shape[0]
    of, at = iota((total // parts, total), 0), iota((total // parts, total), 1)
    whole = tiles[...]
    return jnp.concatenate(
        [mm(hot(at == of * parts + c), whole).astype(BF16) for c in range(parts)], axis=1
    )


STAGES = 8
AXES = (0, 1, 2, 0, 2, 0, 1, 0, 1, 2, 1, 1, 2, 0)


FIRST = ((2, 0), (0, 2), (2, 1), (1, 2), (2, 2), (3, 2), (2, 3))
THEN = ((1, 1), (3, 1), (1, 3), (3, 3), (1, 0), (3, 0), (0, 1), (0, 3))


class Comm:
    def __init__(self, refs):
        (
            self.grads, self.result, self.half_in, self.quarter_in, self.tile_in, self.sent, self.got,
            self.ex_sent, self.ex_got,
        ) = refs
        self.graph, self.dp = lax.axis_index("graph"), lax.axis_index("dp")
        self.core = lax.rem(self.graph, 2)
        self.place = [lax.rem(self.graph // 2, 4), self.graph // 8, self.dp]
        self.spots = [[self.find_spot(axis, k) for k in range(16)] for axis in range(3)]

    def device(self, core, place):
        return (place[1] * 8 + place[0] * 2 + core, place[2])

    def partner(self):
        return self.device(1 - self.core, self.place)

    def peer(self, k):
        where = lax.rem(self.graph + k, 32)
        return where, (where, self.dp)

    def chip(self, dx, dy):
        return lax.rem(self.place[1] + dy, 4) * 4 + lax.rem(self.place[0] + dx, 4)

    def along(self, axis, k):
        place = list(self.place)
        place[axis] = lax.rem(place[axis] + k, 4)
        return place[axis], self.device(self.core, place)

    def over(self, axis, k):
        first, second = [a for a in range(3) if a != axis]
        where = lax.rem(self.place[first] * 4 + self.place[second] + k, 16)
        place = list(self.place)
        place[first], place[second] = where // 4, lax.rem(where, 4)
        return where, self.device(self.core, place)

    def greet(self):
        barrier = pltpu.get_barrier_semaphore()

        def signal(device):
            pl.semaphore_signal(barrier, inc=1, device_id=device, device_id_type=pl.DeviceIdType.MESH)

        def near(k, carry):
            signal(self.peer(k)[1])
            return carry

        def far(k, carry):
            signal(self.over(0, k)[1])
            signal(self.over(1, k)[1])
            return carry

        lax.fori_loop(1, 32, near, 0)
        lax.fori_loop(1, 16, far, 0)

    def greeted(self):
        pl.semaphore_wait(pltpu.get_barrier_semaphore(), 61)

    def copy(self, source, target, sent, got, device):
        pltpu.make_async_remote_copy(
            src_ref=source,
            dst_ref=target,
            send_sem=sent,
            recv_sem=got,
            device_id=device,
            device_id_type=pl.DeviceIdType.MESH,
        ).start()

    def send(self, b, stage, source, target, device):
        self.copy(source, target, self.sent.at[b, stage], self.got.at[b, stage], device)

    def wait_size(self, size, semaphore):
        pltpu.make_async_copy(size, size, semaphore).wait()

    def wait(self, semaphores, b, stage):
        whole, half, full, tiles = (
            self.half_in.at[b], self.quarter_in.at[b, 2], self.quarter_in.at[b, pl.ds(0, 2)], self.tile_in.at[b]
        )
        sizes = (whole, half, full, tiles, tiles, full, half, whole)
        self.wait_size(sizes[stage], semaphores.at[b, stage])

    def spot(self, where):
        at = pl.multiple_of((where // 4) * 16, 16)
        lane = pl.multiple_of(lax.rem(where, 4) * LANES, LANES)
        return at, lane

    def half_rows(self, core):
        return pl.ds(pl.multiple_of(core * 256, 256), 256)

    def quarter_rows(self, at):
        return pl.ds(pl.multiple_of(self.core * 256 + at * 64, 64), 64)

    def find_spot(self, axis, k):
        where, device = self.over(axis, k)
        at, lane = self.spot(where)
        return pl.multiple_of(self.core * 256 + self.place[axis] * 64 + at, 16), lane, device

    def own_spot(self, b, k):
        at, lane, device = self.spots[AXES[b]][k]
        return (pl.ds(at, 16), pl.ds(lane, LANES)), device

    def begin(self, b):
        other = self.half_rows(1 - self.core)
        self.send(b, 0, self.grads.at[b, other], self.half_in.at[b], self.partner())

    def part(self, b, k, half):
        base = self.core * 256 + self.along(AXES[b], k)[0] * 64
        size = 64 if half is None else 32
        return pl.ds(pl.multiple_of(base + (32 if half == 1 else 0), size), size)

    def step1(self, b):
        self.wait(self.got, b, 0)
        mine = self.half_rows(self.core)
        self.grads[b, mine, :] = (self.grads[b, mine, :].astype(F32) + self.half_in[b].astype(F32)).astype(BF16)
        for half, k in ((0, 1), (1, 3)):
            target = self.quarter_in.at[b, 2, pl.ds(half * 32, 32)]
            self.send(b, 1, self.grads.at[b, self.part(b, 2, half)], target, self.along(AXES[b], k)[1])

    def step2(self, b):
        self.wait(self.got, b, 1)
        for half, k in ((0, 1), (1, 3)):
            mine = self.part(b, k, half)
            more = self.quarter_in[b, 2, pl.ds(half * 32, 32), :].astype(F32)
            self.grads[b, mine, :] = (self.grads[b, mine, :].astype(F32) + more).astype(BF16)
            self.send(
                b, 2, self.grads.at[b, self.part(b, k, None)], self.quarter_in.at[b, half], self.along(AXES[b], k)[1]
            )

    def step3(self, b):
        self.wait(self.got, b, 2)
        mine = self.part(b, 0, None)
        total = self.grads[b, mine, :].astype(F32)
        for k in range(2):
            total = total + self.quarter_in[b, k].astype(F32)
        self.grads[b, mine, :] = total.astype(BF16)

        for k in range(1, 16):
            spot, device = self.own_spot(b, k)
            self.send(b, 3, self.grads.at[b, spot[0], spot[1]], self.tile_in.at[b, k - 1], device)

    def step4(self, b):
        self.wait(self.got, b, 3)
        spot, _ = self.own_spot(b, 0)
        total = self.grads[b, spot[0], spot[1]].astype(F32)
        total = total + jnp.sum(self.tile_in[b].astype(F32), axis=0)
        mine = self.result.at[b, spot[0], spot[1]]
        mine[...] = total.astype(BF16)

        for k in range(1, 16):
            self.send(b, 4, mine, mine, self.own_spot(b, k)[1])

    def step5(self, b):
        self.wait(self.got, b, 4)
        mine = self.result.at[b, self.part(b, 0, None)]
        for k in (1, 3):
            self.send(b, 5, mine, mine, self.along(AXES[b], k)[1])

    def step6(self, b):
        self.wait(self.got, b, 5)
        for half, k in ((0, 1), (1, 3)):
            other = self.result.at[b, self.part(b, 4 - k, half)]
            self.send(b, 6, other, other, self.along(AXES[b], k)[1])

    def step7(self, b):
        self.wait(self.got, b, 6)
        mine = self.result.at[b, self.half_rows(self.core)]
        self.send(b, 7, mine, mine, self.partner())

    def step8(self, b):
        self.wait(self.got, b, 7)

    def leave(self, b):
        for stage in range(STAGES):
            self.wait(self.sent, b, stage)

    def run(self, step, blocks):
        steps = (
            self.begin, self.step1, self.step2, self.step3, self.step4, self.step5, self.step6, self.step7, self.step8
        )
        for b in blocks:
            steps[step](b)

    def exchange(self, e, out, into):
        mine = pl.ds(pl.multiple_of(self.graph * 16, 16), 16)
        into[mine, :] = out[mine, :]

        def one(k, carry):
            where, device = self.peer(k)
            theirs = pl.ds(pl.multiple_of(where * 16, 16), 16)
            self.copy(out.at[theirs], into.at[mine], self.ex_sent.at[e], self.ex_got.at[e], device)
            return carry

        lax.fori_loop(1, 32, one, 0)

    def exchanged(self, e, into):
        self.wait_size(into.at[pl.ds(0, 31 * 16)], self.ex_got.at[e])
        self.wait_size(into.at[pl.ds(0, 31 * 16)], self.ex_sent.at[e])


def messages_phase(comm, proj, geometry, geometry_weight, counts, sources, arrived):
    peers = counts.shape[1]
    capacity = 64
    grid_rows, width = proj.shape
    high = geometry_weight[...].astype(BF16)
    low = (geometry_weight[...] - high.astype(F32)).astype(BF16)
    count16 = jnp.broadcast_to(counts[...].astype(F32), (16, peers)).astype(BF16)
    home = comm.graph // 2
    target = arrived.at[pl.ds(pl.multiple_of(comm.graph * capacity, capacity), capacity)]

    def compute(chip):
        start = pl.multiple_of(chip * LANES, LANES)
        at = pl.ds(start, LANES)
        slot = start + iota((1, LANES), 1)
        owner = (start + iota((peers, LANES), 1)) // capacity
        limit = mm(count16, hot(owner == iota((peers, LANES), 0)))[:1]
        live = (slot % capacity).astype(F32) < limit
        index = jnp.where(live, sources[:, at], -1)
        shape = jnp.where(live, geometry[:, at].astype(F32), 0.0).astype(BF16)
        table = jnp.concatenate(row_hot(index, grid_rows), axis=1)
        pre = mm(table, proj[...]) + mm_tn(shape, high) + mm_tn(shape, low)
        where = (chip // 4, pl.ds(pl.multiple_of(lax.rem(chip, 4) * LANES, LANES), LANES))
        comm.grads[where[0], where[1], :] = (pre * sigmoid(pre)).astype(BF16)

    def part(chip, core):
        base = lax.rem(chip, 4) * LANES + core * capacity
        return comm.grads.at[chip // 4, pl.ds(pl.multiple_of(base, capacity), capacity)]

    def send(chip, core):
        comm.copy(
            part(chip, core), target, comm.ex_sent.at[4], comm.ex_got.at[4], (chip * 2 + core, comm.dp)
        )

    for dx, dy in FIRST + THEN:
        chip = comm.chip(dx, dy)
        compute(chip)
        send(chip, 1 - comm.core)
        send(chip, comm.core)
    compute(home)
    send(home, 1 - comm.core)
    target[...] = part(home, comm.core)[...]


def tables_phase(senders, receivers, gather, scatter, extended):
    edges = senders.shape[1]
    nodes = gather.shape[1] - extended

    def step(i, carry):
        at = rows(i, LANES)
        send, recv = senders[:, at], receivers[:, at]
        gather[at, :extended] = jnp.concatenate(row_hot(send, extended), axis=1)
        gather[at, extended:] = jnp.concatenate(row_hot(recv, nodes), axis=1)
        scatter[:extended, at] = hot(iota((extended, LANES), 0) == send)
        scatter[extended:, at] = hot(iota((nodes, LANES), 0) == recv)
        return carry

    lax.fori_loop(0, edges // LANES, step, 0)


def halo_send(comm, e, nodes, picked, out, into):
    pack(mm(picked[...], nodes[...]).astype(BF16), out)
    comm.exchange(e, out, into)


def start_phase(arrived, targets, embed, message_weight, update, output, nodes, total):
    slots = targets.shape[1]
    count, width = embed.shape
    total[...] = jnp.zeros_like(total)

    def step(i, carry):
        at = rows(i, TILE)
        total[...] += mm(hot(iota((count, TILE), 0) == targets[:, at]), arrived[at, :])
        return carry

    lax.fori_loop(0, slots // TILE, step, 0)
    aggregate = mm(total[...].astype(BF16), message_weight[...]).astype(BF16)
    pre = mm(embed[...], update[0]) + mm(aggregate, update[1])
    normed, _ = normalize(mm((pre * sigmoid(pre)).astype(BF16), output[...]))
    nodes[...] = (embed[...].astype(F32) + normed).astype(BF16)


def forward_phase(comm, e, w, nodes, incoming, edges, gather, scatter, saved, new_nodes, proj, total, before):
    count, width = nodes.shape
    extended = gather.shape[1] - count
    proj[:count] = mm(nodes[...], w(WS)).astype(BF16)
    proj[extended:] = mm(nodes[...], w(WR)).astype(BF16)

    def early(i, carry):
        at = rows(i, TILE)
        before[at, :] = (
            mm(edges[at, :], w(WE))
            + mm(gather[at, :count], proj[:count])
            + mm(gather[at, extended:], proj[extended:])
        )
        return carry

    lax.fori_loop(0, edges.shape[0] // TILE, early, 0)
    comm.exchanged(e, incoming)
    proj[count:extended] = mm(unpack(incoming, width), w(WS)).astype(BF16)
    total[...] = jnp.zeros_like(total)

    def step(i, carry):
        at = rows(i, TILE)
        pre = before[at, :] + mm(gather[at, count:extended], proj[count:extended])
        s = sigmoid(pre)
        act = pre * s
        hid = act.astype(BF16)
        saved["hid"][at, :] = hid
        saved["slope"][at, :] = (s + act * (1.0 - s)).astype(BF16)
        normed, inverse = normalize(mm(hid, w(E2)))
        saved["normed"][at, :] = normed.astype(BF16)
        saved["inverse"][0][at, saved["inverse"][1]] = jnp.broadcast_to(inverse, (TILE, LANES // 2))
        new = (edges[at, :].astype(F32) + normed).astype(BF16)
        if saved["edges"] is not None:
            saved["edges"][at, :] = new
        total[...] += mm(scatter[extended:, at], new)
        return carry

    lax.fori_loop(0, edges.shape[0] // TILE, step, 0)
    summed = total[...].astype(BF16)
    pre = mm(nodes[...], w(PV)) + mm(summed, w(PA))
    s = sigmoid(pre)
    act = pre * s
    hid = act.astype(BF16)
    normed, inverse = normalize(mm(hid, w(N2)))
    new_nodes[...] = (nodes[...].astype(F32) + normed).astype(BF16)
    saved["summed"][...] = summed
    saved["node_hid"][...] = hid
    saved["node_slope"][...] = s + act * (1.0 - s)
    saved["node_normed"][...] = normed
    saved["node_inverse"][...] = jnp.broadcast_to(inverse, (count, LANES))


def backward_nodes(put, w, nodes, saved, grad_nodes, proj, extended):
    upstream = grad_nodes[...]
    q = normalize_back(saved["node_normed"][...], saved["node_inverse"][:, :1], upstream)
    q = q.astype(BF16)
    d_node = (mm_nt(q, w(N2)) * saved["node_slope"][...]).astype(BF16)
    proj[extended:] = mm_nt(d_node, w(PA)).astype(BF16)
    put(N2, mm_tn(saved["node_hid"][...], q))
    put(PV, mm_tn(nodes[...], d_node))
    put(PA, mm_tn(saved["summed"][...], d_node))
    grad_nodes[...] = upstream + mm_nt(d_node, w(PV))


def backward_inner(gather, saved, grad_edges, first, last, proj, acc, extended, low, high):
    def step(i, carry):
        at = rows(i, TILE)
        up = mm(gather[at, extended:], proj[extended:])
        if not first:
            up = up + grad_edges[at, :]
        inverse = saved["inverse"][0][at, saved["inverse"][1]][:, :1]
        q = normalize_back(saved["normed"][at, :].astype(F32), inverse, up)
        q = q.astype(BF16)
        acc[...] += mm_tn(saved["hid"][at, :], q)
        saved["hid"][at, :] = q
        if not last:
            grad_edges[at, :] = up
        return carry

    lax.fori_loop(low, high, step, 0)


def backward_outer(w, edges, scatter, saved, total, acc, low, high):
    def step(i, carry):
        at = rows(i, TILE)
        d = (mm_nt(saved["hid"][at, :], w(E2)) * saved["slope"][at, :].astype(F32)).astype(BF16)
        total[...] += mm(scatter[:, at], d)
        if acc is None:
            saved["hid"][at, :] = d
        else:
            acc[...] += mm_tn(edges[at, :], d)
        return carry

    lax.fori_loop(low, high, step, 0)


def backward_rest(w, edges, saved, grad_edges, acc, low, high):
    def step(i, carry):
        at = rows(i, TILE)
        d = saved["hid"][at, :]
        acc[...] += mm_tn(edges[at, :], d)
        grad_edges[at, :] += mm_nt(d, w(WE))
        return carry

    lax.fori_loop(low, high, step, 0)


SAVED = ("hid", "slope", "normed", "edges", "summed", "node_hid", "node_slope", "node_normed", "node_inverse")


def saved_shapes(edges, nodes, width, with_edges):
    shapes = {
        "hid": ((edges, width), BF16),
        "slope": ((edges, width), BF16),
        "normed": ((edges, width), BF16),
        "edges": ((edges, width), BF16),
        "summed": ((nodes, width), BF16),
        "node_hid": ((nodes, width), BF16),
        "node_slope": ((nodes, width), F32),
        "node_normed": ((nodes, width), F32),
        "node_inverse": ((nodes, LANES), F32),
    }
    return [shapes[name] for name in SAVED if with_edges or name != "edges"]


def saved_refs(refs, with_edges):
    names = [name for name in SAVED if with_edges or name != "edges"]
    found = dict(zip(names, refs))
    found.setdefault("edges", None)
    return found


def whole_kernel(
    scale,
    embed, geometry, counts, sources, targets, halo, senders, receivers, geometry_weight, cotangent,
    grid_any, grid_weight_any, message_weight_any, update_any, output_any, edges_any, weights_any,
    nodes2, mesh_gradient, result, *scratch,
):
    scratch = list(scratch)
    take = lambda n: [scratch.pop(0) for _ in range(n)]
    grads, half_in, quarter_in, tile_in, sent, got, ex_sent, ex_got, load = take(9)
    comm = Comm((grads, result, half_in, quarter_in, tile_in, sent, got, ex_sent, ex_got))
    arrived, edges, weights, gather, scatter, picked, nodes0, nodes1 = take(8)
    outs, ins = take(4), take(4)
    grad_edges, grad_nodes, proj, total, summing, acc_inner, acc_outer = take(7)
    saved0 = saved_refs(take(len(SAVED)), True)
    saved1 = saved_refs(take(len(SAVED) - 1), False)
    (inverses,) = take(1)
    saved0["inverse"] = (inverses, slice(0, LANES // 2))
    saved1["inverse"] = (inverses, slice(LANES // 2, LANES))
    count, width = embed.shape
    extended = count + halo.shape[1]
    tiles = edges.shape[0] // TILE
    loads = [
        pltpu.make_async_copy(source, target, load.at[i])
        for i, (source, target) in enumerate(
            (
                (grid_any, grads.at[4]),
                (grid_weight_any, grads.at[5]),
                (message_weight_any, grads.at[6]),
                (output_any, grads.at[7]),
                (update_any, grads.at[pl.ds(8, 2)]),
                (edges_any, edges),
                (weights_any, weights),
            )
        )
    ]
    for copy in loads[:2]:
        copy.start()
    comm.greet()
    for copy in loads[:2]:
        copy.wait()
    for copy in loads[2:]:
        copy.start()
    slots_proj = proj.at[pl.ds(0, grid_any.shape[0])]
    slots_proj[...] = mm(grads[4], grads[5]).astype(BF16)
    comm.greeted()
    messages_phase(comm, slots_proj, geometry, geometry_weight, counts, sources, arrived)
    tables_phase(senders, receivers, gather, scatter, extended)
    picked[...] = jnp.concatenate(row_hot(halo[...], count), axis=1)
    for copy in loads[2:]:
        copy.wait()
    comm.wait_size(arrived.at[pl.ds(0, 31 * 64)], ex_got.at[4])
    start_phase(arrived, targets, embed, grads.at[6], grads.at[pl.ds(8, 2)], grads.at[7], nodes0, summing)
    halo_send(comm, 0, nodes0, picked, outs[0], ins[0])

    def w0(which):
        return weights[block(which, width), :]

    def w1(which):
        return weights[block(7 + which, width), :]

    forward_phase(comm, 0, w0, nodes0, ins[0], edges, gather, scatter, saved0, nodes1, proj, summing, grad_edges)
    halo_send(comm, 1, nodes1, picked, outs[1], ins[1])
    edges1 = saved0["edges"]
    forward_phase(comm, 1, w1, nodes1, ins[1], edges1, gather, scatter, saved1, nodes2, proj, summing, grad_edges)
    grad_nodes[...] = cotangent[...].astype(F32)

    def putter(layer):
        def put(which, value):
            grads[layer * 7 + which] = (value * scale).astype(BF16)

        return put

    def blocks(layer, *which):
        return [layer * 7 + i for i in which]

    run = comm.run

    def clear():
        total[...] = jnp.zeros_like(total)
        acc_inner[...] = jnp.zeros_like(acc_inner)
        acc_outer[...] = jnp.zeros_like(acc_outer)

    def give_back(e):
        pack(total[count:extended].astype(BF16), outs[e])
        comm.exchange(e, outs[e], ins[e])

    def edge_sums(put, w, nodes, layer, incoming):
        recv = total[extended:].astype(BF16)
        put(WR, mm_tn(nodes[...], recv))
        run(0, blocks(layer, WR))
        outer16 = total[count:extended].astype(BF16)
        put(WS, mm_tn(nodes[...], total[:count].astype(BF16)) + mm_tn(unpack(incoming, width), outer16))
        run(0, blocks(layer, WS))
        grad_nodes[...] += mm_nt(recv, w(WR))

    def finish(w, e):
        comm.exchanged(e, ins[e])
        back = hot(iota((count, halo.shape[1]), 0) == halo[...])
        send = (total[:count] + mm(back, unpack(ins[e], width))).astype(BF16)
        grad_nodes[...] += mm_nt(send, w(WS))

    put1, put0 = putter(1), putter(0)
    a1, e1, b1 = blocks(1, N2, PV, PA), blocks(1, E2), blocks(1, WE, WR, WS)
    a0, e0, b0 = blocks(0, N2, PV, PA), blocks(0, E2), blocks(0, WE, WR, WS)
    comm.wait_size(arrived.at[pl.ds(0, 31 * 64)], ex_sent.at[4])

    pieces = [(i * tiles // 3, (i + 1) * tiles // 3) for i in range(3)]

    def inner(piece, saved, first, last):
        backward_inner(gather, saved, grad_edges, first, last, proj, acc_inner, extended, *pieces[piece])

    def outer(piece, w, edges, saved, acc):
        backward_outer(w, edges, scatter, saved, total, acc, *pieces[piece])

    def rest(piece):
        backward_rest(w1, edges1, saved1, grad_edges, acc_outer, *pieces[piece])

    clear()
    backward_nodes(put1, w1, nodes1, saved1, grad_nodes, proj, extended)
    run(0, a1)
    inner(0, saved1, True, False)
    inner(1, saved1, True, False)
    inner(2, saved1, True, False)
    put1(E2, acc_inner[...])
    run(0, e1)
    run(1, a1)
    outer(0, w1, edges1, saved1, None)
    outer(1, w1, edges1, saved1, None)
    run(1, e1)
    outer(2, w1, edges1, saved1, None)
    run(2, a1)
    give_back(2)
    run(2, e1)
    rest(0)
    rest(1)
    rest(2)
    put1(WE, acc_outer[...])
    run(0, blocks(1, WE))
    edge_sums(put1, w1, nodes1, 1, ins[1])
    run(3, a1)
    finish(w1, 2)
    clear()
    backward_nodes(put0, w0, nodes0, saved0, grad_nodes, proj, extended)
    run(0, a0)
    run(1, b1)
    run(3, e1)
    inner(0, saved0, False, True)
    inner(1, saved0, False, True)
    inner(2, saved0, False, True)
    put0(E2, acc_inner[...])
    run(0, e0)
    run(1, a0)
    run(4, a1)
    outer(0, w0, edges, saved0, acc_outer)
    run(2, b1)
    run(4, e1)
    outer(1, w0, edges, saved0, acc_outer)
    run(1, e0)
    outer(2, w0, edges, saved0, acc_outer)
    run(2, a0)
    put0(WE, acc_outer[...])
    run(0, blocks(0, WE))
    edge_sums(put0, w0, nodes0, 0, ins[0])
    give_back(3)
    run(2, e0)
    run(1, b0)
    run(3, b1)
    run(5, a1)
    run(5, e1)
    run(3, a0)
    finish(w0, 3)
    mesh_gradient[...] = grad_nodes[...].astype(BF16)
    run(2, b0)
    run(4, b1)
    run(3, e0)
    run(6, a1)
    run(6, e1)
    run(3, b0)
    run(4, a0)
    run(4, e0)
    run(7, a1)
    run(7, e1)
    run(5, b1)
    run(4, b0)
    run(5, a0)
    run(5, e0)
    run(6, b1)
    run(5, b0)
    run(6, a0)
    run(6, e0)
    run(7, b1)
    run(6, b0)
    run(7, a0)
    run(7, e0)
    run(7, b0)
    run(8, range(14))
    for b in range(14):
        comm.leave(b)


def on_device(
    grid_latent,
    mesh_embed,
    mesh_edges,
    edge_geometry,
    edge_counts,
    edge_sources,
    edge_targets,
    halo_sources,
    mesh_sources,
    mesh_targets,
    grid_weight,
    geometry_weight,
    message_weight,
    mesh_update,
    mesh_output,
    processor,
    cotangent,
):
    count, width = mesh_embed.shape
    edges = mesh_edges.shape[0]
    slots = edge_sources.shape[1]
    halo = halo_sources.shape[1]
    peers = lax.axis_size("graph")
    extended = count + halo
    table = extended + count
    tiles = (halo * width // LANES, LANES)
    scale = 1.0 / math.sqrt(lax.axis_size("dp") * peers * count)
    layers = processor.shape[0]
    vmem, anywhere = pl.BlockSpec(memory_space=pltpu.VMEM), pl.BlockSpec(memory_space=pl.ANY)
    dma = pltpu.SemaphoreType.DMA
    scratch = [
        ((7 * layers, width, width), BF16),
        ((7 * layers, width // 2, width), BF16),
        ((7 * layers, 3, width // 8, width), BF16),
        ((7 * layers, 15, 16, LANES), BF16),
        dma((7 * layers, STAGES)),
        dma((7 * layers, STAGES)),
        dma((5,)),
        dma((5,)),
        dma((7,)),
        ((slots, width), BF16),
        ((edges, width), BF16),
        ((7 * layers * width, width), BF16),
        ((edges, table), BF16),
        ((table, edges), BF16),
        ((halo, count), BF16),
        ((count, width), BF16),
        ((count, width), BF16),
        *[(tiles, BF16)] * 8,
        ((edges, width), F32),
        ((count, width), F32),
        ((table, width), BF16),
        ((table, width), F32),
        ((count, width), F32),
        ((width, width), F32),
        ((width, width), F32),
        *saved_shapes(edges, count, width, True),
        *saved_shapes(edges, count, width, False),
        ((edges, LANES), F32),
    ]
    nodes2, result, gradients = pl.pallas_call(
        functools.partial(whole_kernel, scale),
        out_shape=[
            pltpu.VMEM((count, width), BF16),
            pltpu.VMEM((count, width), BF16),
            pltpu.VMEM((7 * layers, width, width), BF16),
        ],
        in_specs=[vmem] * 10 + [anywhere] * 7,
        out_specs=[vmem] * 3,
        scratch_shapes=[pltpu.VMEM(*item) if isinstance(item, tuple) else item for item in scratch],
        compiler_params=pltpu.CompilerParams(
            collective_id=0, has_side_effects=True, vmem_limit_bytes=59100000
        ),
    )(
        mesh_embed, edge_geometry[0], edge_counts, edge_sources, edge_targets, halo_sources, mesh_sources,
        mesh_targets, geometry_weight, cotangent[0],
        grid_latent[0], grid_weight, message_weight, mesh_update.reshape(2, width, width), mesh_output,
        mesh_edges, processor.reshape(-1, width),
    )
    return nodes2[None], result[None], gradients.reshape(processor.shape)


def solution(mesh):
    in_specs = (
        P("dp", "graph", None),
        P("graph", None),
        P("graph", None),
        P("graph", None, None),
        P("graph", None),
        P("graph", None),
        P("graph", None),
        P("graph", None),
        P("graph", None),
        P("graph", None),
        P(),
        P(),
        P(),
        P(),
        P(),
        P(),
        P("dp", "graph", None),
    )
    out_specs = (P("dp", "graph", None), P("dp", "graph", None), P())
    return jax.shard_map(
        on_device, mesh=mesh, in_specs=in_specs, out_specs=out_specs, check_vma=False
    )
```
